32 devices in a mesh: gx: 2 (over y), gy: 4 (over z), gz: 4 (over x, core).
Axes of the slice: x: 2, y: 2, z: 4, core: 2. Of those that a mesh axis runs over, the one named last changes fastest.
Arguments:
- moments: float32 [32, 128, 16, 128], P('gx', ('gy', 'gz')), may hold values from -128 to 128, as said below
- stiffness: float32 [32, 128, 16], P('gx', ('gy', 'gz')), may hold values from 0.5 to 4
- damping: float32 [32, 128, 16], P('gx', ('gy', 'gz')), may hold values from 0.05 to 1
- density: float32 [32, 128, 16], P('gx', ('gy', 'gz')), may hold values from 0.5 to 1.5
- ritz_coeffs: float32 [128, 128], replicated, may hold values from -128 to 128
- shifts: float32 [128], replicated, may hold values from -1.5 to -0.3
Outputs:
- ritz_vectors: float32 [32, 128, 16, 128], P('gx', ('gy', 'gz'))
- ritz_residual: float32 [32, 128, 16, 128], P('gx', ('gy', 'gz'))
- stiff_proj: float32 [128, 128], replicated
- damp_proj: float32 [128, 128], replicated
- mass_proj: float32 [128, 128], replicated
- first_factor: float32 [128, 128], replicated
The draws below stay inside these ranges and needn't reach their ends.
Inputs may be any that keep to these rules, and one draw needn't show every extreme that they name: `moments`: A real block of full column rank.
All inputs are finite; a program needn't handle non-finite values.
Results may differ from the reference program's by a relative error of at most 0.0004.
Values sent between devices are 32-bit elements; how exact they have to be, the bound alone decides.
A program may use at most 64 MiB of HBM per device.

```python
import math
import jax
import jax.numpy as jnp
from jax import lax

COLS = 128
NZ = 16
NX = 32
NY = 128


def draw_moments(key, part):
    key_own = jax.random.fold_in(key, 11)
    key_common = jax.random.fold_in(key, 23)
    key_scale = jax.random.fold_in(key, 37)
    own = jax.random.truncated_normal(key_own, -4.0, 4.0, (NX, NY, NZ, COLS), jnp.float32)
    common = jax.random.truncated_normal(key_common, -4.0, 4.0, (NX, NY, NZ, 1), jnp.float32)
    scales = jnp.exp(jax.random.uniform(key_scale, (COLS,), jnp.float32, 0.0, math.log(10.0)))
    weight_own = 0.01
    ramp = 1.0 + 2.0 * jnp.arange(NX, dtype=jnp.float32) / (NX - 1)
    return ramp.reshape(NX, 1, 1, 1) * scales * (common + weight_own * own)


def steps_of(stream_key, extent, pieces, low, largest):
    loudness, own = 1.0, jax.random.fold_in(stream_key, 6)
    for dim, parts in pieces:
        draws = jnp.exp(jax.random.uniform(jax.random.fold_in(own, dim), (parts,), jnp.float32, low / len(pieces), largest / len(pieces)))
        loudness = loudness * jnp.repeat(draws, extent[dim] // parts).reshape([-1 if axis == dim else 1 for axis in range(len(extent))])
    return loudness


def centred(key, shape, width, reach, kind=jnp.bfloat16):
    return jnp.clip(width * jax.random.normal(key, shape, jnp.float32), -reach, reach).astype(kind)


def setup_inputs(seed: int = 0) -> dict:
    splits = jax.random.split(jax.random.key(seed), 7)
    moments = draw_moments(jax.random.fold_in(splits[6], 71), 0)
    stiffness = jnp.clip(jnp.exp(math.log(4.0) - 2.0794415 * jax.random.uniform(splits[1], (NX, NY, NZ), jnp.float32) ** steps_of(splits[1], (NX, NY, NZ), ((0, 2), (1, 16)), -0.2, 0.2)), 0.5, 4.0)
    damping = jnp.clip(jnp.exp(math.log(1.0) - 2.9957323 * jax.random.uniform(splits[2], (NX, NY, NZ), jnp.float32) ** steps_of(splits[2], (NX, NY, NZ), ((0, 2), (1, 16)), -0.2, 0.2)), 0.05, 1.0)
    density = jnp.clip(0.5 + 1.0 * jax.random.uniform(splits[3], (NX, NY, NZ), jnp.float32) ** steps_of(splits[3], (NX, NY, NZ), ((0, 2), (1, 16)), -0.2, 0.2), 0.5, 1.5)
    ritz_coeffs = centred(splits[4], (COLS, COLS), ((NX * NY * NZ / COLS) ** 0.5), 128.0, jnp.float32)
    shifts = jnp.clip(jax.random.uniform(splits[5], (COLS,), jnp.float32, -1.5, -0.3), -1.5, -0.3)
    return dict(moments=moments, stiffness=stiffness, damping=damping, density=density, ritz_coeffs=ritz_coeffs, shifts=shifts)


def factorize(gram):
    count = gram.shape[0]
    index = jnp.arange(count, dtype=jnp.int32)

    def column_step(j, carry):
        work, lower = carry
        onehot = (index == j).astype(gram.dtype)
        column = lax.optimization_barrier(jnp.sum(work * onehot[None, :], axis=1))
        pivot = jnp.sum(column * onehot)
        column = jnp.where(index >= j, column, jnp.zeros_like(column)) / jnp.sqrt(pivot)
        lower = lower + column[:, None] * onehot[None, :]
        work = work - column[:, None] * column[None, :]
        return (work, lower)
    start = (gram, jnp.zeros_like(gram))
    lower = lax.fori_loop(0, count, column_step, start)[1]

    def row_step(i, inverse):
        onehot = (index == i).astype(gram.dtype)
        row = lax.optimization_barrier(jnp.sum(lower * onehot[:, None], axis=0))
        pivot = jnp.sum(row * onehot)
        rhs = onehot - lax.optimization_barrier(jnp.sum(row[:, None] * inverse, axis=0))
        return inverse + onehot[:, None] * (rhs / pivot)[None, :]
    inverse = lax.fori_loop(0, count, row_step, jnp.zeros_like(gram))
    return (lower, inverse.T)

def neighbours(field):
    padded = jnp.pad(field, ((1, 1), (1, 1), (1, 1), (0, 0)))
    total = padded[2:, 1:-1, 1:-1] + padded[:-2, 1:-1, 1:-1]
    total = total + padded[1:-1, 2:, 1:-1] + padded[1:-1, :-2, 1:-1]
    total = total + padded[1:-1, 1:-1, 2:] + padded[1:-1, 1:-1, :-2]
    return total

def reference(moments, stiffness, damping, density, ritz_coeffs, shifts):
    highest = lax.Precision.HIGHEST
    cells = NX * NY * NZ
    flat = moments.reshape(cells, COLS)
    lower_one, first_inv = factorize(jnp.dot(flat.T, flat, precision=highest))
    first_factor = lower_one.T / jnp.sqrt(jnp.float32(cells))
    basis_one = jnp.dot(flat, first_inv, precision=highest)
    second_inv = factorize(jnp.dot(basis_one.T, basis_one, precision=highest))[1]
    basis = jnp.dot(basis_one, second_inv, precision=highest)
    near = neighbours(basis.reshape(NX, NY, NZ, COLS)).reshape(cells, COLS)
    stiff_col = stiffness.reshape(cells, 1)
    damp_col = damping.reshape(cells, 1)
    dens_col = density.reshape(cells, 1)
    k_block = (6.0 + stiff_col) * basis - near
    c_block = damp_col * basis
    m_block = dens_col * basis + near / 12.0
    stiff_proj = jnp.dot(basis.T, k_block, precision=highest)
    damp_proj = jnp.dot(basis.T, c_block, precision=highest)
    mass_proj = jnp.dot(basis.T, m_block, precision=highest)
    ritz = jnp.dot(basis, ritz_coeffs, precision=highest)
    resid = jnp.dot(k_block, ritz_coeffs, precision=highest)
    resid = resid + jnp.dot(c_block, ritz_coeffs, precision=highest) * shifts
    resid = resid + jnp.dot(m_block, ritz_coeffs, precision=highest) * (shifts * shifts)
    return (ritz.reshape(NX, NY, NZ, COLS), resid.reshape(NX, NY, NZ, COLS), stiff_proj, damp_proj, mass_proj, first_factor)
```

```python
import functools
import math
import jax
import jax.numpy as jnp
from jax import lax
from jax.experimental import pallas as pl
from jax.experimental.pallas import tpu as pltpu
from jax.sharding import PartitionSpec as P

MESH = pl.DeviceIdType.MESH
HI = lax.Precision.HIGHEST
F32 = jnp.float32
BF16 = jnp.bfloat16
BLK = 16


def mm(a, b):
    return lax.dot_general(a, b, (((1,), (0,)), ((), ())), precision=HI, preferred_element_type=F32)


def mm_t(a, b):
    return lax.dot_general(a, b, (((0,), (0,)), ((), ())), precision=HI, preferred_element_type=F32)


def split(x):
    high = x.astype(BF16)
    return high, (x - high.astype(F32)).astype(BF16)


def split3(x):
    high = x.astype(BF16)
    rest = x - high.astype(F32)
    mid = rest.astype(BF16)
    return high, mid, (rest - mid.astype(F32)).astype(BF16)


def dot_t(a, b):
    return lax.dot_general(a, b, (((0,), (0,)), ((), ())), preferred_element_type=F32)


def dot(a, b):
    return lax.dot_general(a, b, (((1,), (0,)), ((), ())), preferred_element_type=F32)


def rank_update(a, b):
    ah, am, al = split3(a)
    bh, bm, bl = split3(b)
    left = jnp.concatenate([ah, am, ah, am, ah, al], axis=0)
    right = jnp.concatenate([bh, bh, bm, bm, bl, bh], axis=0)
    return dot_t(left, right)


def coeff_tile(c):
    high, low = split(c)
    return jnp.concatenate(
        [jnp.concatenate([high, low], axis=1), jnp.concatenate([high, jnp.zeros_like(high)], axis=1)], axis=0
    )


def mm_three(rows, tile):
    w = rows.shape[1]
    out = dot(jnp.concatenate(split(rows), axis=1), tile)
    return out[:, :w] + out[:, w:]


def inv_tiles(c):
    high, mid, low = split3(c)
    pair = jnp.concatenate([high, mid], axis=1)
    return jnp.concatenate([pair, pair], axis=0), jnp.concatenate([low, high], axis=0)


def mm_six(rows, tiles):
    w = rows.shape[1]
    high, mid, low = split3(rows)
    one = dot(jnp.concatenate([high, mid], axis=1), tiles[0])
    two = dot(jnp.concatenate([high, low], axis=1), tiles[1])
    return (two + one[:, w:]) + one[:, :w]


def stencil(pad, x, by, zero):
    q = pad[x + 1, 1 : by + 1]
    near = pad[x, 1 : by + 1] + pad[x + 2, 1 : by + 1]
    near = near + pad[x + 1, 0:by] + pad[x + 1, 2 : by + 2]
    near = near + jnp.concatenate([q[:, 1:], zero], axis=1)
    near = near + jnp.concatenate([zero, q[:, :-1]], axis=1)
    return q, near


def field(cells, f, dx, by, bz, w):
    part = cells[f * bz : (f + 1) * bz]
    return jnp.stack([jnp.broadcast_to(part[:, dx * by + y : dx * by + y + 1], (bz, w)) for y in range(by)])


def factorize(work, upper, inverse, between=None):
    n = work.shape[0]
    lane = lax.broadcasted_iota(jnp.int32, (BLK, n), 1)
    sub = lax.broadcasted_iota(jnp.int32, (BLK, n), 0)
    lane_all = lax.broadcasted_iota(jnp.int32, (n, n), 1)

    def block(jb, carry):
        first = pl.multiple_of(jb * BLK, BLK)
        rows = work[pl.ds(first, BLK), :]
        cols = [
            jnp.broadcast_to(
                jnp.sum(jnp.where(lane == first + k, rows, 0.0), axis=1, keepdims=True), (BLK, n)
            )
            for k in range(BLK)
        ]
        u = jnp.where(lane >= first, rows, 0.0)
        e = jnp.where(lane < first, rows, jnp.where(lane == first + sub, 1.0, 0.0))
        pivots = jnp.zeros((BLK, n), F32)
        for s in range(BLK):
            pivot = jnp.broadcast_to(cols[s][s : s + 1], (BLK, n))
            pivots = jnp.where(sub == s, pivot, pivots)
            if s == BLK - 1:
                break
            m = jnp.where(sub > s, cols[s] / pivot, 0.0)
            for k in range(s + 1, BLK):
                cols[k] = cols[k] - m * cols[k][s : s + 1]
            u = u - m * u[s : s + 1]
            e = e - m * e[s : s + 1]
        scale = 1.0 / jnp.sqrt(pivots)
        u = jnp.where(lane >= first + sub, u * scale, 0.0)
        e = e * scale
        upper[pl.ds(first, BLK), :] = u
        inverse[pl.ds(first, BLK), :] = e
        beyond = jnp.where(lane >= first + BLK, u, 0.0)
        panel = (lane_all >= first) & (lane_all < first + BLK)
        work[...] = jnp.where(panel, 0.0, work[...]) - rank_update(beyond, beyond + e)
        return carry

    late = n // BLK // 2
    lax.fori_loop(0, late, block, 0)
    result = between() if between else None
    lax.fori_loop(late, n // BLK, block, 0)
    return result


def kernel(
    sizes,
    y_hbm, stiff_in, damp_in, dens_in, ritz_in, shifts_in,
    vec_out, res_out, proj_out, factor_out,
    pad, cells_ref, proj, inv_b,
    y_ref, ys, qs, fields, spread, diag, ritz_ref, shifts_ref, halo_x, halo_y, work, upper, inv_a,
    g_src, g_recv, g_z, g_full, h_src, h_recv, h_z, h_full, p_src, p_recv, p_z, p_full, load_sem,
    halo_send, halo_got, a_send, a_got, z_send, z_got, b_send, b_got,
):
    nx, ny, nz, all_cells = sizes
    bx, by, bz, w = y_ref.shape
    group, levels = g_recv.shape[0], g_z.shape[0]
    count = g_src.shape[0]
    ix, iy, iz = lax.axis_index("gx"), lax.axis_index("gy"), lax.axis_index("gz")
    mine = ix * nz + iz
    level = iy
    line = iy * nz + iz
    owners = owner_places(nx, nz)
    stride = group // count
    is_owner = lax.rem(iz, stride) == stride - 1
    my_part = lax.div(mine, stride)

    def plane_id(a):
        return (a // nz, iy, a % nz)

    def line_id(a):
        return (ix, lax.div(a, nz), lax.rem(a, nz))

    sides = [
        (ix > 0, (ix - 1, iy, iz), y_ref.at[0], halo_x.at[1], halo_x.at[0]),
        (ix < nx - 1, (ix + 1, iy, iz), y_ref.at[bx - 1], halo_x.at[0], halo_x.at[1]),
        (line > 0, line_id(line - 1), y_ref.at[:, 0], halo_y.at[1], halo_y.at[0]),
        (line < ny * nz - 1, line_id(line + 1), y_ref.at[:, by - 1], halo_y.at[0], halo_y.at[1]),
    ]
    planes = [lax.rem(iy + d, ny) for d in range(1, levels)]

    parts = 4
    px = bx // parts
    loads = [
        pltpu.make_async_copy(y_hbm.at[pl.ds(i * px, px)], y_ref.at[pl.ds(i * px, px)], load_sem.at[i])
        for i in range(parts)
    ]
    for f, src in enumerate((stiff_in, damp_in, dens_in)):
        loads.append(pltpu.make_async_copy(src, fields.at[f], load_sem.at[parts + f]))
    loads.append(pltpu.make_async_copy(ritz_in, ritz_ref, load_sem.at[parts + 3]))
    loads.append(pltpu.make_async_copy(shifts_in, shifts_ref, load_sem.at[parts + 4]))
    for load in loads:
        load.start()

    barrier = pltpu.get_barrier_semaphore()
    expected = jnp.int32(0)
    for a in range(group):
        talks = mine != a
        if a not in owners:
            talks = talks & is_owner
        expected = expected + talks.astype(jnp.int32)

        @pl.when(talks)
        def _():
            pl.semaphore_signal(barrier, inc=1, device_id=plane_id(a), device_id_type=MESH)

    @pl.when(is_owner)
    def _():
        for plane in planes:
            pl.semaphore_signal(barrier, inc=1, device_id=(ix, plane, iz), device_id_type=MESH)

    expected = expected + jnp.where(is_owner, levels - 1, 0)
    for exists, device, _, _, _ in sides:
        expected = expected + exists.astype(jnp.int32)

        @pl.when(exists)
        def _():
            pl.semaphore_signal(barrier, inc=1, device_id=device, device_id_type=MESH)

    cross = jnp.zeros((2 * w, 2 * w), F32)
    third_order = jnp.zeros((w, w), F32)
    n_rows = px * by * bz
    for i in range(parts):
        loads[i].wait()
        high, mid, low = split3(y_ref[i * px : (i + 1) * px].reshape(n_rows, w))
        two = jnp.concatenate([mid, high], axis=1)
        ys[i * n_rows : (i + 1) * n_rows, : 2 * w] = two
        ys[i * n_rows : (i + 1) * n_rows, 2 * w :] = low
        cross = cross + dot_t(two, two)
        third_order = third_order + dot_t(high, low)
    small = cross[:w, w:] + third_order
    work[...] = cross[w:, w:] + (cross[:w, :w] + (small + small.T))

    pl.semaphore_wait(barrier, expected)

    def halo_copy(k):
        _, device, src, dst, _ = sides[k]
        other = k ^ 1
        return pltpu.make_async_remote_copy(
            src_ref=src, dst_ref=dst, send_sem=halo_send.at[k], recv_sem=halo_got.at[other],
            device_id=device, device_id_type=MESH,
        )

    def to_owner(slot, o, src, recv, place):
        return pltpu.make_async_remote_copy(
            src_ref=src.at[o], dst_ref=recv.at[place], send_sem=a_send.at[slot, o],
            recv_sem=a_got.at[slot, place], device_id=plane_id(owners[o]), device_id_type=MESH,
        )

    def to_plane(slot, d, z):
        return pltpu.make_async_remote_copy(
            src_ref=z.at[level], dst_ref=z.at[level], send_sem=z_send.at[slot, d],
            recv_sem=z_got.at[slot, d], device_id=(ix, planes[d], iz), device_id_type=MESH,
        )

    def from_owner(slot, a, full, part):
        return pltpu.make_async_remote_copy(
            src_ref=full.at[part], dst_ref=full.at[part], send_sem=b_send.at[slot, a],
            recv_sem=b_got.at[slot, part], device_id=plane_id(a), device_id_type=MESH,
        )

    def each_owner(fn):
        for o in range(count):
            @pl.when(mine != owners[o])
            def _():
                fn(o)

    def each_place(fn):
        for a in range(group):
            @pl.when(mine != a)
            def _():
                fn(a)

    def reduce_start(slot, src, recv):
        each_owner(lambda o: to_owner(slot, o, src, recv, mine).start())

    def level_start(slot, src, recv, z):
        @pl.when(is_owner)
        def _():
            each_place(lambda a: to_owner(slot, 0, src, recv, a).wait_recv())
            recv[mine] = src[my_part]
            total = recv[0]
            for a in range(1, group):
                total = total + recv[a]
            z[level] = total
            for d in range(levels - 1):
                to_plane(slot, d, z).start()

    def gather_start(slot, z, full):
        @pl.when(is_owner)
        def _():
            for d in range(levels - 1):
                to_plane(slot, d, z).wait_recv()
            total = z[0]
            for d in range(1, levels):
                total = total + z[d]
            full[my_part] = total
            each_place(lambda a: from_owner(slot, a, full, my_part).start())

    def gather_end(slot, full, out):
        each_owner(lambda o: from_owner(slot, 0, full, o).wait_recv())
        r = full.shape[1]
        for o in range(count):
            out[o * r : (o + 1) * r, :] = full[o]

    def drain(slot, src, recv, z, full):
        each_owner(lambda o: to_owner(slot, o, src, recv, mine).wait_send())

        @pl.when(is_owner)
        def _():
            for d in range(levels - 1):
                to_plane(slot, d, z).wait_send()
            each_place(lambda a: from_owner(slot, a, full, my_part).wait_send())

    def chunks(src, out):
        r = out.shape[1]
        for o in range(count):
            out[o] = src[o * r : (o + 1) * r, :]

    chunks(work, g_src)
    reduce_start(0, g_src, g_recv)

    empty = jnp.zeros((bx * by, w - 3 * bz), F32)
    for load in loads[parts:]:
        load.wait()
    cells_ref[...] = jnp.concatenate([fields[0], fields[1], fields[2], empty], axis=1).T
    lanes = bx * by
    shifts = shifts_ref[...].reshape(1, 1, w)
    squares = shifts * shifts

    def spread_step(i, carry):
        cells = pltpu.roll(cells_ref[0 : 3 * bz, :], lax.rem(lanes - i * 2 * by, lanes), 1)
        for dx in range(2):
            k_field = 6.0 + field(cells, 0, dx, by, bz, w)
            c_field = field(cells, 1, dx, by, bz, w)
            m_field = field(cells, 2, dx, by, bz, w)
            spread[0, i * 2 + dx] = k_field
            spread[1, i * 2 + dx] = c_field
            spread[2, i * 2 + dx] = m_field
            diag[i * 2 + dx] = k_field + c_field * shifts + m_field * squares
        return carry

    lax.fori_loop(0, bx // 2, spread_step, 0)

    level_start(0, g_src, g_recv, g_z)
    gather_start(0, g_z, g_full)
    gather_end(0, g_full, work)
    for k, (exists, _, _, _, land) in enumerate(sides):
        @pl.when(exists)
        def _():
            halo_copy(k).start()

        @pl.when(jnp.logical_not(exists))
        def _():
            land[...] = jnp.zeros(land.shape, F32)
    factorize(work, upper, inv_a)
    factor_out[...] = upper[...] / math.sqrt(all_cells)
    tiles = inv_tiles(inv_a[...].T)

    def basis_step(i, total):
        at = pl.multiple_of(i * n_rows, n_rows)
        one = dot(ys[pl.ds(at, n_rows), : 2 * w], tiles[0])
        two = dot(ys[pl.ds(at, n_rows), w:], tiles[1])
        q = (two + one[:, w:]) + one[:, :w]
        pad[pl.ds(i * px + 1, px), 1 : by + 1] = q.reshape(px, by, bz, w)
        high, low = split(q)
        both = jnp.concatenate([high, low], axis=1)
        qs[pl.ds(at, n_rows), :] = both
        return total + dot_t(high, both)

    pair = lax.fori_loop(0, parts, basis_step, jnp.zeros((w, 2 * w), F32))
    small = pair[:, w:]
    work[...] = pair[:, :w] + (small + small.T)
    chunks(work, h_src)
    reduce_start(1, h_src, h_recv)

    for k, (exists, _, _, _, _) in enumerate(sides):
        @pl.when(exists)
        def _():
            halo_copy(k).wait_send()
            halo_copy(k ^ 1).wait_recv()
    for side, at in ((0, 0), (1, bx + 1)):
        pad[at, 1 : by + 1] = mm_six(halo_x[side].reshape(by * bz, w), tiles).reshape(by, bz, w)
    for side, at in ((0, 0), (1, by + 1)):
        pad[1 : bx + 1, at] = mm_six(halo_y[side].reshape(bx * bz, w), tiles).reshape(bx, bz, w)
    for at_x in (0, bx + 1):
        for at_y in (0, by + 1):
            pad[at_x, at_y] = jnp.zeros((bz, w), F32)

    zero = jnp.zeros((by, 1, w), F32)
    proj[...] = jnp.zeros(proj.shape, F32)
    p_rows = 2 * by * bz

    def proj_step(i, carry):
        wides = []
        for dx in range(2):
            q, near = stencil(pad, i * 2 + dx, by, zero)
            k_block = spread[0, i * 2 + dx] * q - near
            c_block = spread[1, i * 2 + dx] * q
            m_block = spread[2, i * 2 + dx] * q + near * (1.0 / 12.0)
            wides.append(jnp.concatenate([v.reshape(by * bz, w) for v in (k_block, c_block, m_block)], axis=1))
        both = qs[pl.ds(pl.multiple_of(i * p_rows, p_rows), p_rows), :]
        qh, ql = both[:, :w], both[:, w:]
        vh, vl = split(jnp.concatenate(wides, axis=0))
        out = dot_t(ql, vh) + dot_t(qh, vl) + dot_t(qh, vh)
        for p in range(3):
            proj[p * w : (p + 1) * w, :] += out[:, p * w : (p + 1) * w]
        return carry

    steps = bx // 2
    cut = steps * 5 // 8
    lax.fori_loop(0, cut, proj_step, 0)
    level_start(1, h_src, h_recv, h_z)
    lax.fori_loop(cut, steps, proj_step, 0)
    chunks(proj, p_src)
    reduce_start(2, p_src, p_recv)
    gather_start(1, h_z, h_full)
    gather_end(1, h_full, work)
    factorize(work, upper, inv_b, lambda: level_start(2, p_src, p_recv, p_z))
    tile = coeff_tile(mm(inv_b[...].T, ritz_ref[...]))

    def vector_step(i, carry):
        rows = pad[pl.ds(i * 2, 2)].reshape(2 * (by + 2) * bz, w)
        pad[pl.ds(i * 2, 2)] = mm_three(rows, tile).reshape(2, by + 2, bz, w)
        return carry

    near_scale = squares * (1.0 / 12.0) - 1.0

    def residual_step(i, carry):
        for dx in range(2):
            v, near = stencil(pad, i * 2 + dx, by, zero)
            vec_out[i * 2 + dx] = v
            res_out[i * 2 + dx] = diag[i * 2 + dx] * v + near_scale * near
        return carry

    lax.fori_loop(0, (bx + 2) // 2, vector_step, 0)
    lax.fori_loop(0, bx // 2, residual_step, 0)
    gather_start(2, p_z, p_full)
    drain(0, g_src, g_recv, g_z, g_full)
    drain(1, h_src, h_recv, h_z, h_full)
    gather_end(2, p_full, proj)
    left = inv_b[...]
    half = mm(proj[...], left.T)
    out = mm(left, jnp.concatenate([half[p * w : (p + 1) * w] for p in range(3)], axis=1))
    for p in range(3):
        proj_out[p * w : (p + 1) * w, :] = out[:, p * w : (p + 1) * w]
    drain(2, p_src, p_recv, p_z, p_full)


def owner_places(nx, nz):
    stride = 2 if nz % 2 == 0 else 1
    return [a for a in range(nx * nz) if a % nz % stride == stride - 1]


def finish(
    vec_in, res_in, proj_in, factor_in,
    vec_ref, res_ref, stiff_ref, damp_ref, mass_ref, factor_ref,
    sems,
):
    w = factor_ref.shape[0]
    pairs = [(vec_in, vec_ref), (res_in, res_ref), (factor_in, factor_ref)]
    for p, ref in enumerate((stiff_ref, damp_ref, mass_ref)):
        pairs.append((proj_in.at[pl.ds(p * w, w)], ref))
    copies = [pltpu.make_async_copy(a, b, sems.at[i]) for i, (a, b) in enumerate(pairs)]
    for copy in copies:
        copy.start()
    for copy in copies:
        copy.wait()


def local(sizes, moments, stiffness, damping, density, ritz_coeffs, shifts):
    nx, ny, nz, _ = sizes
    bx, by, bz, w = moments.shape
    group, levels = nx * nz, ny
    count = len(owner_places(nx, nz))
    flat = [f.reshape(bx * by, bz) for f in (stiffness, damping, density)]
    r = w // count
    q = 3 * w // count
    mat = jax.ShapeDtypeStruct((w, w), F32)
    block = jax.ShapeDtypeStruct(moments.shape, F32)
    square = pltpu.VMEM((w, w), F32)
    hbm = pl.BlockSpec(memory_space=pltpu.HBM)
    vmem = pl.BlockSpec(memory_space=pltpu.VMEM)
    dma = pltpu.SemaphoreType.DMA
    padded = (bx + 2, by + 2, bz, w)

    def stages(rows):
        return [
            pltpu.VMEM((count, rows, w), F32),
            pltpu.VMEM((group, rows, w), F32),
            pltpu.VMEM((levels, rows, w), F32),
            pltpu.VMEM((count, rows, w), F32),
        ]

    shared = pl.pallas_call(
        functools.partial(kernel, sizes),
        out_shape=(
            pltpu.VMEM(moments.shape, F32), pltpu.VMEM(moments.shape, F32),
            pltpu.VMEM((3 * w, w), F32), pltpu.VMEM((w, w), F32),
        ),
        in_specs=[hbm] * 6,
        out_specs=(vmem,) * 4,
        scratch_shapes=[
            pltpu.VMEM(padded, F32),
            square,
            pltpu.VMEM((3 * w, w), F32),
            square,
            pltpu.VMEM(moments.shape, F32),
            pltpu.VMEM((bx * by * bz, 3 * w), BF16),
            pltpu.VMEM((bx * by * bz, 2 * w), BF16),
            pltpu.VMEM((3, bx * by, bz), F32),
            pltpu.VMEM((3,) + moments.shape, F32),
            pltpu.VMEM(moments.shape, F32),
            square,
            pltpu.VMEM((1, w), F32),
            pltpu.VMEM((2, by, bz, w), F32),
            pltpu.VMEM((2, bx, bz, w), F32),
            square, square, square,
            *stages(r), *stages(r), *stages(q),
            dma((9,)),
            dma((4,)), dma((4,)),
            dma((3, count)), dma((3, group)),
            dma((3, max(levels - 1, 1))), dma((3, max(levels - 1, 1))),
            dma((3, group)), dma((3, count)),
        ],
        compiler_params=pltpu.CompilerParams(
            collective_id=0, has_side_effects=True, vmem_limit_bytes=32 << 20
        ),
    )(*(pltpu.with_memory_space_constraint(a, pltpu.HBM) for a in (moments, *flat, ritz_coeffs, shifts.reshape(1, w))))
    any_space = pl.BlockSpec(memory_space=pl.ANY)
    return pl.pallas_call(
        finish,
        out_shape=(block, block, mat, mat, mat, mat),
        in_specs=[any_space] * 4,
        out_specs=(hbm,) * 6,
        scratch_shapes=[dma((6,))],
        compiler_params=pltpu.CompilerParams(vmem_limit_bytes=1 << 20),
    )(*shared)


def solution(mesh):
    nx, ny, nz = (mesh.shape[a] for a in ("gx", "gy", "gz"))

    def call(moments, *rest):
        cells = moments.shape[0] * moments.shape[1] * moments.shape[2]
        body = functools.partial(local, (nx, ny, nz, cells * nx * ny * nz))
        return body(moments, *rest)

    cube = P("gx", ("gy", "gz"), None)
    block = P("gx", ("gy", "gz"), None, None)
    return jax.shard_map(
        call,
        mesh=mesh,
        in_specs=(block, cube, cube, cube, P(), P()),
        out_specs=(block, block, P(), P(), P(), P()),
        check_vma=False,
    )
```

```python
import functools
import math
import jax
import jax.numpy as jnp
from jax import lax
from jax.experimental import pallas as pl
from jax.experimental.pallas import tpu as pltpu
from jax.sharding import PartitionSpec as P

MESH = pl.DeviceIdType.MESH
HI = lax.Precision.HIGHEST
F32 = jnp.float32
BF16 = jnp.bfloat16
BLK = 16


def mm(a, b):
    return lax.dot_general(a, b, (((1,), (0,)), ((), ())), precision=HI, preferred_element_type=F32)


def mm_t(a, b):
    return lax.dot_general(a, b, (((0,), (0,)), ((), ())), precision=HI, preferred_element_type=F32)


def split(x):
    high = x.astype(BF16)
    return high, (x - high.astype(F32)).astype(BF16)


def split3(x):
    high = x.astype(BF16)
    rest = x - high.astype(F32)
    mid = rest.astype(BF16)
    return high, mid, (rest - mid.astype(F32)).astype(BF16)


def dot_t(a, b):
    return lax.dot_general(a, b, (((0,), (0,)), ((), ())), preferred_element_type=F32)


def dot(a, b):
    return lax.dot_general(a, b, (((1,), (0,)), ((), ())), preferred_element_type=F32)


def rank_update(a, b):
    ah, am, al = split3(a)
    bh, bm, bl = split3(b)
    left = jnp.concatenate([ah, am, ah, am, ah, al], axis=0)
    right = jnp.concatenate([bh, bh, bm, bm, bl, bh], axis=0)
    return dot_t(left, right)


def coeff_tile(c):
    high, low = split(c)
    return jnp.concatenate(
        [jnp.concatenate([high, low], axis=1), jnp.concatenate([high, jnp.zeros_like(high)], axis=1)], axis=0
    )


def mm_three(rows, tile):
    w = rows.shape[1]
    out = dot(jnp.concatenate(split(rows), axis=1), tile)
    return out[:, :w] + out[:, w:]


def inv_tiles(c):
    high, mid, low = split3(c)
    pair = jnp.concatenate([high, mid], axis=1)
    return jnp.concatenate([pair, pair], axis=0), jnp.concatenate([low, high], axis=0)


def mm_six(rows, tiles):
    w = rows.shape[1]
    high, mid, low = split3(rows)
    one = dot(jnp.concatenate([high, mid], axis=1), tiles[0])
    two = dot(jnp.concatenate([high, low], axis=1), tiles[1])
    return (two + one[:, w:]) + one[:, :w]


def stencil(pad, x, by, zero):
    q = pad[x + 1, 1 : by + 1]
    near = pad[x, 1 : by + 1] + pad[x + 2, 1 : by + 1]
    near = near + pad[x + 1, 0:by] + pad[x + 1, 2 : by + 2]
    near = near + jnp.concatenate([q[:, 1:], zero], axis=1)
    near = near + jnp.concatenate([zero, q[:, :-1]], axis=1)
    return q, near


def field(cells, f, dx, by, bz, w):
    part = cells[f * bz : (f + 1) * bz]
    return jnp.stack([jnp.broadcast_to(part[:, dx * by + y : dx * by + y + 1], (bz, w)) for y in range(by)])


def factorize(work, upper, inverse, between=None):
    n = work.shape[0]
    lane = lax.broadcasted_iota(jnp.int32, (BLK, n), 1)
    sub = lax.broadcasted_iota(jnp.int32, (BLK, n), 0)
    lane_all = lax.broadcasted_iota(jnp.int32, (n, n), 1)

    def block(jb, carry):
        first = pl.multiple_of(jb * BLK, BLK)
        rows = work[pl.ds(first, BLK), :]
        cols = [
            jnp.broadcast_to(
                jnp.sum(jnp.where(lane == first + k, rows, 0.0), axis=1, keepdims=True), (BLK, n)
            )
            for k in range(BLK)
        ]
        u = jnp.where(lane >= first, rows, 0.0)
        e = jnp.where(lane < first, rows, jnp.where(lane == first + sub, 1.0, 0.0))
        pivots = jnp.zeros((BLK, n), F32)
        for s in range(BLK):
            pivot = jnp.broadcast_to(cols[s][s : s + 1], (BLK, n))
            pivots = jnp.where(sub == s, pivot, pivots)
            if s == BLK - 1:
                break
            m = jnp.where(sub > s, cols[s] / pivot, 0.0)
            for k in range(s + 1, BLK):
                cols[k] = cols[k] - m * cols[k][s : s + 1]
            u = u - m * u[s : s + 1]
            e = e - m * e[s : s + 1]
        scale = 1.0 / jnp.sqrt(pivots)
        u = jnp.where(lane >= first + sub, u * scale, 0.0)
        e = e * scale
        upper[pl.ds(first, BLK), :] = u
        inverse[pl.ds(first, BLK), :] = e
        beyond = jnp.where(lane >= first + BLK, u, 0.0)
        panel = (lane_all >= first) & (lane_all < first + BLK)
        work[...] = jnp.where(panel, 0.0, work[...]) - rank_update(beyond, beyond + e)
        return carry

    late = n // BLK // 2
    lax.fori_loop(0, late, block, 0)
    result = between() if between else None
    lax.fori_loop(late, n // BLK, block, 0)
    return result


def halves(h, w):
    row = lax.broadcasted_iota(jnp.int32, (h, w), 0)
    lane = lax.broadcasted_iota(jnp.int32, (h, w), 1)
    return row, lane


def pack(g):
    w = g.shape[0]
    h = w // 2
    row, lane = halves(h, w)
    top, low = g[:h], g[h:]
    turned = pltpu.roll(low, h, 1)
    body = jnp.where((lane >= h) | (row >= lane), top, turned)
    ends = jnp.where(row == lane, turned, 0.0) + jnp.where(row == lane - h, low, 0.0)
    return body, jnp.sum(ends, axis=0, keepdims=True)


def unpack(body, ends):
    h, w = body.shape
    row, lane = halves(h, w)
    flipped = jnp.concatenate([body, body], axis=0).T
    top = jnp.where((lane >= h) | (row >= lane), body, flipped[:h])
    last = jnp.where(row == lane - h, jnp.broadcast_to(ends, (h, w)), flipped[:h])
    last = jnp.where(row < lane - h, pltpu.roll(body, h, 1), last)
    return jnp.concatenate([top, jnp.where(lane < h, flipped[h:], last)], axis=0)


def each(n, fn):
    if n <= 64:
        for g in range(n):
            fn(g)
    else:
        def step(g, carry):
            fn(g)
            return carry

        lax.fori_loop(0, n, step, 0)


def add_up(terms):
    while len(terms) > 1:
        pairs = [terms[i] + terms[i + 1] for i in range(0, len(terms) - 1, 2)]
        terms = pairs + terms[len(pairs) * 2 :]
    return terms[0]


class Owners:
    def __init__(self, nx, ny, nz):
        self.stride = 2 if nz % 2 == 0 else 1
        self.span = 2 if ny % 2 == 0 else 1
        self.first = (ny - self.span) // 2
        self.nz, self.group = nz, nx * nz
        self.in_plane = self.group // self.stride
        self.count = self.span * self.in_plane
        self.devices = self.group * ny

    def holds(self, iy, iz):
        middle = (iy >= self.first) & (iy < self.first + self.span)
        return middle & (lax.rem(iz, self.stride) == self.stride - 1)

    def part(self, iy, mine):
        return (iy - self.first) * self.in_plane + lax.div(mine, self.stride)

    def device(self, o):
        plane = self.first + o // self.in_plane
        return plane * self.group + o % self.in_plane * self.stride + self.stride - 1

    def place(self, g):
        a = g % self.group
        return (a // self.nz, g // self.group, a % self.nz)


def kernel(
    sizes,
    y_hbm, stiff_in, damp_in, dens_in, ritz_in, shifts_in,
    vec_out, res_out, proj_out, factor_out,
    pad, cells_ref, proj, inv_b,
    y_ref, ys, qs, fields, spread, diag, ritz_ref, shifts_ref, halo_x, halo_y, work, upper, inv_a,
    g_src, g_recv, g_full, h_src, h_recv, h_full, p_src, p_recv, p_full, load_sem,
    halo_send, halo_got, a_send, a_got, b_send, b_got,
):
    nx, ny, nz, all_cells = sizes
    bx, by, bz, w = y_ref.shape
    ix, iy, iz = lax.axis_index("gx"), lax.axis_index("gy"), lax.axis_index("gz")
    owners = Owners(nx, ny, nz)
    devices, count = owners.devices, owners.count
    mine = ix * nz + iz
    me = iy * owners.group + mine
    line = iy * nz + iz
    is_owner = owners.holds(iy, iz)
    my_part = owners.part(iy, mine)

    def line_id(a):
        return (ix, lax.div(a, nz), lax.rem(a, nz))

    sides = [
        (ix > 0, (ix - 1, iy, iz), y_ref.at[0], halo_x.at[1], halo_x.at[0]),
        (ix < nx - 1, (ix + 1, iy, iz), y_ref.at[bx - 1], halo_x.at[0], halo_x.at[1]),
        (line > 0, line_id(line - 1), y_ref.at[:, 0], halo_y.at[1], halo_y.at[0]),
        (line < ny * nz - 1, line_id(line + 1), y_ref.at[:, by - 1], halo_y.at[0], halo_y.at[1]),
    ]

    parts = 4
    px = bx // parts
    loads = [
        pltpu.make_async_copy(y_hbm.at[pl.ds(i * px, px)], y_ref.at[pl.ds(i * px, px)], load_sem.at[i])
        for i in range(parts)
    ]
    for f, src in enumerate((stiff_in, damp_in, dens_in)):
        loads.append(pltpu.make_async_copy(src, fields.at[f], load_sem.at[parts + f]))
    loads.append(pltpu.make_async_copy(ritz_in, ritz_ref, load_sem.at[parts + 3]))
    loads.append(pltpu.make_async_copy(shifts_in, shifts_ref, load_sem.at[parts + 4]))
    for load in loads:
        load.start()

    barrier = pltpu.get_barrier_semaphore()
    def greet(g):
        pl.semaphore_signal(barrier, inc=1, device_id=owners.place(g), device_id_type=MESH)

    def greet_owner(o):
        @pl.when(me != owners.device(o))
        def _():
            greet(owners.device(o))

    def greet_all(g):
        @pl.when(me != g)
        def _():
            greet(g)

    @pl.when(is_owner)
    def _():
        each(devices, greet_all)

    @pl.when(jnp.logical_not(is_owner))
    def _():
        each(count, greet_owner)

    expected = jnp.where(is_owner, devices - 1, count)
    for exists, device, _, _, _ in sides:
        expected = expected + exists.astype(jnp.int32)

        @pl.when(exists)
        def _():
            pl.semaphore_signal(barrier, inc=1, device_id=device, device_id_type=MESH)

    cross = jnp.zeros((2 * w, 2 * w), F32)
    third_order = jnp.zeros((w, w), F32)
    n_rows = px * by * bz
    for i in range(parts):
        loads[i].wait()
        high, mid, low = split3(y_ref[i * px : (i + 1) * px].reshape(n_rows, w))
        two = jnp.concatenate([mid, high], axis=1)
        ys[i * n_rows : (i + 1) * n_rows, : 2 * w] = two
        ys[i * n_rows : (i + 1) * n_rows, 2 * w :] = low
        cross = cross + dot_t(two, two)
        third_order = third_order + dot_t(high, low)
    small = cross[:w, w:] + third_order
    gram = cross[w:, w:] + (cross[:w, :w] + (small + small.T))

    pl.semaphore_wait(barrier, expected)

    def halo_copy(k):
        _, device, src, dst, _ = sides[k]
        other = k ^ 1
        return pltpu.make_async_remote_copy(
            src_ref=src, dst_ref=dst, send_sem=halo_send.at[k], recv_sem=halo_got.at[other],
            device_id=device, device_id_type=MESH,
        )

    def to_owner(slot, o, src, recv, sender):
        return pltpu.make_async_remote_copy(
            src_ref=src.at[o], dst_ref=recv.at[sender], send_sem=a_send.at[slot, o],
            recv_sem=a_got.at[slot, sender], device_id=owners.place(owners.device(o)), device_id_type=MESH,
        )

    def from_owner(slot, g, full, part):
        return pltpu.make_async_remote_copy(
            src_ref=full.at[part], dst_ref=full.at[part], send_sem=b_send.at[slot, g],
            recv_sem=b_got.at[slot, part], device_id=owners.place(g), device_id_type=MESH,
        )

    def each_owner(fn):
        def other(o):
            @pl.when(me != owners.device(o))
            def _():
                fn(o)

        each(count, other)

    def each_device(fn):
        def other(g):
            @pl.when(me != g)
            def _():
                fn(g)

        each(devices, other)

    def reduce_start(slot, mats, src, recv):
        k = len(mats)
        r = mats[0].shape[0] // 2 // count
        for p, mat in enumerate(mats):
            body, ends = pack(mat)
            for o in range(count):
                src[o, p * r : (p + 1) * r, :] = body[o * r : (o + 1) * r]
                src[o, k * r + p : k * r + p + 1, :] = ends
        each_owner(lambda o: to_owner(slot, o, src, recv, me).start())

    def gather_start(slot, src, recv, full):
        @pl.when(is_owner)
        def _():
            recv[me] = src[my_part]
            each_device(lambda g: to_owner(slot, 0, src, recv, g).wait_recv())
            full[my_part] = add_up([recv[g] for g in range(devices)])
            each_device(lambda g: from_owner(slot, g, full, my_part).start())

    def gather_end(slot, k, full):
        each_owner(lambda o: from_owner(slot, 0, full, o).wait_recv())
        r = full.shape[1] // k
        out = []
        for p in range(k):
            body = jnp.concatenate([full[o, p * (r - 1) : (p + 1) * (r - 1), :] for o in range(count)], axis=0)
            out.append(unpack(body, full[0, k * (r - 1) + p : k * (r - 1) + p + 1, :]))
        return out

    def drain(slot, src, recv, full):
        each_owner(lambda o: to_owner(slot, o, src, recv, me).wait_send())

        @pl.when(is_owner)
        def _():
            each_device(lambda g: from_owner(slot, g, full, my_part).wait_send())

    reduce_start(0, [gram], g_src, g_recv)

    empty = jnp.zeros((bx * by, w - 3 * bz), F32)
    for load in loads[parts:]:
        load.wait()
    cells_ref[...] = jnp.concatenate([fields[0], fields[1], fields[2], empty], axis=1).T
    lanes = bx * by
    shifts = shifts_ref[...].reshape(1, 1, w)
    squares = shifts * shifts

    def spread_step(i, carry):
        cells = pltpu.roll(cells_ref[0 : 3 * bz, :], lax.rem(lanes - i * 2 * by, lanes), 1)
        for dx in range(2):
            k_field = 6.0 + field(cells, 0, dx, by, bz, w)
            c_field = field(cells, 1, dx, by, bz, w)
            m_field = field(cells, 2, dx, by, bz, w)
            spread[0, i * 2 + dx] = k_field
            spread[1, i * 2 + dx] = c_field
            spread[2, i * 2 + dx] = m_field
            diag[i * 2 + dx] = k_field + c_field * shifts + m_field * squares
        return carry

    lax.fori_loop(0, bx // 2, spread_step, 0)

    gather_start(0, g_src, g_recv, g_full)
    work[...] = gather_end(0, 1, g_full)[0]
    for k, (exists, _, _, _, land) in enumerate(sides):
        @pl.when(exists)
        def _():
            halo_copy(k).start()

        @pl.when(jnp.logical_not(exists))
        def _():
            land[...] = jnp.zeros(land.shape, F32)
    factorize(work, upper, inv_a)
    factor_out[...] = upper[...] / math.sqrt(all_cells)
    tiles = inv_tiles(inv_a[...].T)

    def basis_step(i, total):
        at = pl.multiple_of(i * n_rows, n_rows)
        one = dot(ys[pl.ds(at, n_rows), : 2 * w], tiles[0])
        two = dot(ys[pl.ds(at, n_rows), w:], tiles[1])
        q = (two + one[:, w:]) + one[:, :w]
        pad[pl.ds(i * px + 1, px), 1 : by + 1] = q.reshape(px, by, bz, w)
        high, low = split(q)
        both = jnp.concatenate([high, low], axis=1)
        qs[pl.ds(at, n_rows), :] = both
        return total + dot_t(high, both)

    pair = lax.fori_loop(0, parts, basis_step, jnp.zeros((w, 2 * w), F32))
    small = pair[:, w:]
    reduce_start(1, [pair[:, :w] + (small + small.T)], h_src, h_recv)

    for k, (exists, _, _, _, _) in enumerate(sides):
        @pl.when(exists)
        def _():
            halo_copy(k).wait_send()
            halo_copy(k ^ 1).wait_recv()
    for side, at in ((0, 0), (1, bx + 1)):
        pad[at, 1 : by + 1] = mm_six(halo_x[side].reshape(by * bz, w), tiles).reshape(by, bz, w)
    for side, at in ((0, 0), (1, by + 1)):
        pad[1 : bx + 1, at] = mm_six(halo_y[side].reshape(bx * bz, w), tiles).reshape(bx, bz, w)
    for at_x in (0, bx + 1):
        for at_y in (0, by + 1):
            pad[at_x, at_y] = jnp.zeros((bz, w), F32)

    zero = jnp.zeros((by, 1, w), F32)
    proj[...] = jnp.zeros(proj.shape, F32)
    p_rows = 2 * by * bz

    def proj_step(i, carry):
        wides = []
        for dx in range(2):
            q, near = stencil(pad, i * 2 + dx, by, zero)
            k_block = spread[0, i * 2 + dx] * q - near
            c_block = spread[1, i * 2 + dx] * q
            m_block = spread[2, i * 2 + dx] * q + near * (1.0 / 12.0)
            wides.append(jnp.concatenate([v.reshape(by * bz, w) for v in (k_block, c_block, m_block)], axis=1))
        both = qs[pl.ds(pl.multiple_of(i * p_rows, p_rows), p_rows), :]
        qh, ql = both[:, :w], both[:, w:]
        vh, vl = split(jnp.concatenate(wides, axis=0))
        out = dot_t(ql, vh) + dot_t(qh, vl) + dot_t(qh, vh)
        for p in range(3):
            proj[p * w : (p + 1) * w, :] += out[:, p * w : (p + 1) * w]
        return carry

    steps = bx // 2
    cut = steps * 7 // 8
    lax.fori_loop(0, cut, proj_step, 0)
    gather_start(1, h_src, h_recv, h_full)
    lax.fori_loop(cut, steps, proj_step, 0)
    reduce_start(2, [proj[p * w : (p + 1) * w, :] for p in range(3)], p_src, p_recv)
    work[...] = gather_end(1, 1, h_full)[0]
    factorize(work, upper, inv_b, lambda: gather_start(2, p_src, p_recv, p_full))
    tile = coeff_tile(mm(inv_b[...].T, ritz_ref[...]))

    def vector_step(i, carry):
        rows = pad[pl.ds(i * 2, 2)].reshape(2 * (by + 2) * bz, w)
        pad[pl.ds(i * 2, 2)] = mm_three(rows, tile).reshape(2, by + 2, bz, w)
        return carry

    near_scale = squares * (1.0 / 12.0) - 1.0

    def residual_step(i, carry):
        for dx in range(2):
            v, near = stencil(pad, i * 2 + dx, by, zero)
            vec_out[i * 2 + dx] = v
            res_out[i * 2 + dx] = diag[i * 2 + dx] * v + near_scale * near
        return carry

    lax.fori_loop(0, (bx + 2) // 2, vector_step, 0)
    lax.fori_loop(0, bx // 2, residual_step, 0)
    drain(0, g_src, g_recv, g_full)
    drain(1, h_src, h_recv, h_full)
    sums = gather_end(2, 3, p_full)
    left = inv_b[...]
    half = mm(jnp.concatenate(sums, axis=0), left.T)
    out = mm(left, jnp.concatenate([half[p * w : (p + 1) * w] for p in range(3)], axis=1))
    for p in range(3):
        proj_out[p * w : (p + 1) * w, :] = out[:, p * w : (p + 1) * w]
    drain(2, p_src, p_recv, p_full)


def finish(
    vec_in, res_in, proj_in, factor_in,
    vec_ref, res_ref, stiff_ref, damp_ref, mass_ref, factor_ref,
    sems,
):
    w = factor_ref.shape[0]
    pairs = [(vec_in, vec_ref), (res_in, res_ref), (factor_in, factor_ref)]
    for p, ref in enumerate((stiff_ref, damp_ref, mass_ref)):
        pairs.append((proj_in.at[pl.ds(p * w, w)], ref))
    copies = [pltpu.make_async_copy(a, b, sems.at[i]) for i, (a, b) in enumerate(pairs)]
    for copy in copies:
        copy.start()
    for copy in copies:
        copy.wait()


def local(sizes, moments, stiffness, damping, density, ritz_coeffs, shifts):
    nx, ny, nz, _ = sizes
    bx, by, bz, w = moments.shape
    owners = Owners(nx, ny, nz)
    devices, count = owners.devices, owners.count
    flat = [f.reshape(bx * by, bz) for f in (stiffness, damping, density)]
    r = w // 2 // count + 1
    mat = jax.ShapeDtypeStruct((w, w), F32)
    block = jax.ShapeDtypeStruct(moments.shape, F32)
    square = pltpu.VMEM((w, w), F32)
    hbm = pl.BlockSpec(memory_space=pltpu.HBM)
    vmem = pl.BlockSpec(memory_space=pltpu.VMEM)
    dma = pltpu.SemaphoreType.DMA
    padded = (bx + 2, by + 2, bz, w)

    def stages(rows):
        return [
            pltpu.VMEM((count, rows, w), F32),
            pltpu.VMEM((devices, rows, w), F32),
            pltpu.VMEM((count, rows, w), F32),
        ]

    shared = pl.pallas_call(
        functools.partial(kernel, sizes),
        out_shape=(
            pltpu.VMEM(moments.shape, F32), pltpu.VMEM(moments.shape, F32),
            pltpu.VMEM((3 * w, w), F32), pltpu.VMEM((w, w), F32),
        ),
        in_specs=[hbm] * 6,
        out_specs=(vmem,) * 4,
        scratch_shapes=[
            pltpu.VMEM(padded, F32),
            square,
            pltpu.VMEM((3 * w, w), F32),
            square,
            pltpu.VMEM(moments.shape, F32),
            pltpu.VMEM((bx * by * bz, 3 * w), BF16),
            pltpu.VMEM((bx * by * bz, 2 * w), BF16),
            pltpu.VMEM((3, bx * by, bz), F32),
            pltpu.VMEM((3,) + moments.shape, F32),
            pltpu.VMEM(moments.shape, F32),
            square,
            pltpu.VMEM((1, w), F32),
            pltpu.VMEM((2, by, bz, w), F32),
            pltpu.VMEM((2, bx, bz, w), F32),
            square, square, square,
            *stages(r), *stages(r), *stages(3 * r),
            dma((9,)),
            dma((4,)), dma((4,)),
            dma((3, count)), dma((3, devices)),
            dma((3, devices)), dma((3, count)),
        ],
        compiler_params=pltpu.CompilerParams(
            collective_id=0, has_side_effects=True, vmem_limit_bytes=32 << 20
        ),
    )(*(pltpu.with_memory_space_constraint(a, pltpu.HBM) for a in (moments, *flat, ritz_coeffs, shifts.reshape(1, w))))
    any_space = pl.BlockSpec(memory_space=pl.ANY)
    return pl.pallas_call(
        finish,
        out_shape=(block, block, mat, mat, mat, mat),
        in_specs=[any_space] * 4,
        out_specs=(hbm,) * 6,
        scratch_shapes=[dma((6,))],
        compiler_params=pltpu.CompilerParams(vmem_limit_bytes=1 << 20),
    )(*shared)


def solution(mesh):
    nx, ny, nz = (mesh.shape[a] for a in ("gx", "gy", "gz"))

    def call(moments, *rest):
        cells = moments.shape[0] * moments.shape[1] * moments.shape[2]
        body = functools.partial(local, (nx, ny, nz, cells * nx * ny * nz))
        return body(moments, *rest)

    cube = P("gx", ("gy", "gz"), None)
    block = P("gx", ("gy", "gz"), None, None)
    return jax.shard_map(
        call,
        mesh=mesh,
        in_specs=(block, cube, cube, cube, P(), P()),
        out_specs=(block, block, P(), P(), P(), P()),
        check_vma=False,
    )
```

```python
import functools
import math
import jax
import jax.numpy as jnp
from jax import lax
from jax.experimental import pallas as pl
from jax.experimental.pallas import tpu as pltpu
from jax.sharding import PartitionSpec as P

MESH = pl.DeviceIdType.MESH
HI = lax.Precision.HIGHEST
F32 = jnp.float32
BF16 = jnp.bfloat16
BLK = 32
PANEL = 16


def mm(a, b):
    return lax.dot_general(a, b, (((1,), (0,)), ((), ())), precision=HI, preferred_element_type=F32)


def split(x):
    high = x.astype(BF16)
    return high, (x - high.astype(F32)).astype(BF16)


def split3(x):
    high = x.astype(BF16)
    rest = x - high.astype(F32)
    mid = rest.astype(BF16)
    return high, mid, (rest - mid.astype(F32)).astype(BF16)


def dot_t(a, b):
    return lax.dot_general(a, b, (((0,), (0,)), ((), ())), preferred_element_type=F32)


def dot(a, b):
    return lax.dot_general(a, b, (((1,), (0,)), ((), ())), preferred_element_type=F32)


def rank_update(a, b):
    ah, am, al = split3(a)
    bh, bm, bl = split3(b)
    left = jnp.concatenate([ah, am, ah, am, ah, al], axis=0)
    right = jnp.concatenate([bh, bh, bm, bm, bl, bh], axis=0)
    return dot_t(left, right)


def mm_t_three(a, b):
    ah, al = split(a)
    bh, bl = split(b)
    return dot_t(jnp.concatenate([ah, ah, al], axis=0), jnp.concatenate([bh, bl, bh], axis=0))


def coeff_tile(c):
    high, low = split(c)
    return jnp.concatenate(
        [jnp.concatenate([high, low], axis=1), jnp.concatenate([high, jnp.zeros_like(high)], axis=1)], axis=0
    )


def inv_tiles(c):
    high, mid, low = split3(c)
    pair = jnp.concatenate([high, mid], axis=1)
    return jnp.concatenate([pair, pair], axis=0), jnp.concatenate([low, high], axis=0)


def mm_six(rows, tiles):
    w = rows.shape[1]
    high, mid, low = split3(rows)
    one = dot(jnp.concatenate([high, mid], axis=1), tiles[0])
    two = dot(jnp.concatenate([high, low], axis=1), tiles[1])
    return (two + one[:, w:]) + one[:, :w]


def stencil(pad, x, by, zero):
    q = pad[x + 1, 1 : by + 1]
    near = pad[x, 1 : by + 1] + pad[x + 2, 1 : by + 1]
    near = near + pad[x + 1, 0:by] + pad[x + 1, 2 : by + 2]
    near = near + jnp.concatenate([q[:, 1:], zero], axis=1)
    near = near + jnp.concatenate([zero, q[:, :-1]], axis=1)
    return q, near


def field(cells, f, dx, by, bz, w):
    part = cells[f * bz : (f + 1) * bz]
    return jnp.stack([jnp.broadcast_to(part[:, dx * by + y : dx * by + y + 1], (bz, w)) for y in range(by)])


def eliminate(a, first):
    nr, n = a.shape
    lane = lax.broadcasted_iota(jnp.int32, (nr, n), 1)
    row = lax.broadcasted_iota(jnp.int32, (nr, n), 0)
    cols = [jnp.broadcast_to(a[:, first + k : first + k + 1], (nr, n)) for k in range(PANEL)]
    inside = (lane >= first) & (lane < first + PANEL)
    rest = jnp.where(inside, jnp.where(lane == first + row, 1.0, 0.0), a)
    lane, sub = lane[:PANEL], row[:PANEL]
    recips = jnp.zeros((PANEL, n), F32)
    for s in range(PANEL):
        recip = 1.0 / cols[s][s : s + 1]
        recips = jnp.where(sub == s, recip, recips)
        if s == nr - 1:
            break
        m = jnp.where(row > s, cols[s], 0.0) * recip
        for k in range(s + 1, PANEL):
            cols[k] = cols[k] - m * cols[k][s : s + 1]
        rest = rest - m * rest[s : s + 1]
    done = rest[:PANEL]
    e = jnp.where(lane < first + PANEL, done, 0.0)
    u = jnp.where(lane >= first + PANEL, done, 0.0)
    for k in range(PANEL):
        u = jnp.where((lane == first + k) & (sub <= k), cols[k][:PANEL], u)
    return u, e, recips, rest[PANEL:]


def factorize(g, between=None):
    n = g.shape[0]
    blocks = n // BLK
    rows = [g[b * BLK : (b + 1) * BLK] for b in range(blocks)]
    upper, inverse = [], []
    lane = lax.broadcasted_iota(jnp.int32, (BLK, n), 1)
    for j in range(blocks):
        first = j * BLK
        a = rows[j]
        parts = []
        for p in range(BLK // PANEL):
            u, e, recips, a = eliminate(a, first + p * PANEL)
            parts.append((u, e, recips))
        u, e, recips = (jnp.concatenate(x, axis=0) for x in zip(*parts))
        if j < blocks - 1:
            beyond = jnp.where(lane >= first + BLK, u, 0.0)
            update = rank_update(beyond * recips, beyond + e)
            inside = (lane >= first) & (lane < first + BLK)
            for b in range(j + 1, blocks):
                rows[b] = jnp.where(inside, 0.0, rows[b]) - update[b * BLK : (b + 1) * BLK]
        scale = jnp.sqrt(recips)
        upper.append(u * scale)
        inverse.append(e * scale)
        if between and j == 0:
            between()
    return jnp.concatenate(upper, axis=0), jnp.concatenate(inverse, axis=0)


def halves(h, w):
    row = lax.broadcasted_iota(jnp.int32, (h, w), 0)
    lane = lax.broadcasted_iota(jnp.int32, (h, w), 1)
    return row, lane


def pack(g):
    w = g.shape[0]
    h = w // 2
    row, lane = halves(h, w)
    top, low = g[:h], g[h:]
    turned = pltpu.roll(low, h, 1)
    body = jnp.where((lane >= h) | (row >= lane), top, turned)
    ends = jnp.where(row == lane, turned, 0.0) + jnp.where(row == lane - h, low, 0.0)
    return body, jnp.sum(ends, axis=0, keepdims=True)


def unpack(body, ends):
    h, w = body.shape
    row, lane = halves(h, w)
    flipped = jnp.concatenate([body, body], axis=0).T
    top = jnp.where((lane >= h) | (row >= lane), body, flipped[:h])
    last = jnp.where(row == lane - h, jnp.broadcast_to(ends, (h, w)), flipped[:h])
    last = jnp.where(row < lane - h, pltpu.roll(body, h, 1), last)
    return jnp.concatenate([top, jnp.where(lane < h, flipped[h:], last)], axis=0)


def matrices(k, full):
    count = full.shape[0]
    r = full.shape[1] // k - 1
    out = []
    for p in range(k):
        body = jnp.concatenate([full[o, p * r : (p + 1) * r, :] for o in range(count)], axis=0)
        out.append(unpack(body, full[0, k * r + p : k * r + p + 1, :]))
    return out


def each(n, fn):
    if n <= 64:
        for g in range(n):
            fn(g)
    else:
        def step(g, carry):
            fn(g)
            return carry

        lax.fori_loop(0, n, step, 0)


def add_up(terms):
    while len(terms) > 1:
        pairs = [terms[i] + terms[i + 1] for i in range(0, len(terms) - 1, 2)]
        terms = pairs + terms[len(pairs) * 2 :]
    return terms[0]


class Owners:
    def __init__(self, nx, ny, nz):
        self.stride = 2 if nz % 2 == 0 else 1
        self.span = 2 if ny % 2 == 0 else 1
        self.first = (ny - self.span) // 2
        self.nz, self.group = nz, nx * nz
        self.in_plane = self.group // self.stride
        self.count = self.span * self.in_plane
        self.devices = self.group * ny

    def holds(self, iy, iz):
        middle = (iy >= self.first) & (iy < self.first + self.span)
        return middle & (lax.rem(iz, self.stride) == self.stride - 1)

    def part(self, iy, mine):
        return (iy - self.first) * self.in_plane + lax.div(mine, self.stride)

    def device(self, o):
        plane = self.first + o // self.in_plane
        return plane * self.group + o % self.in_plane * self.stride + self.stride - 1

    def place(self, g):
        a = g % self.group
        return (a // self.nz, g // self.group, a % self.nz)


def kernel(
    sizes,
    y_hbm, stiff_in, damp_in, dens_in, ritz_in, shifts_in,
    vec_out, res_out, proj_out, inv_out, factor_out,
    pad, cells_ref, proj,
    y_ref, ys, qs, hs, fields, spread, diag, ritz_ref, shifts_ref, halo_x, halo_y,
    g_src, g_recv, g_full, h_src, h_recv, h_full, p_src, p_recv, p_full, load_sem,
    halo_send, halo_got, a_send, a_got, b_send, b_got,
):
    nx, ny, nz, all_cells = sizes
    bx, by, bz, w = y_ref.shape
    ix, iy, iz = lax.axis_index("gx"), lax.axis_index("gy"), lax.axis_index("gz")
    owners = Owners(nx, ny, nz)
    devices, count = owners.devices, owners.count
    mine = ix * nz + iz
    me = iy * owners.group + mine
    line = iy * nz + iz
    is_owner = owners.holds(iy, iz)
    my_part = owners.part(iy, mine)

    def line_id(a):
        return (ix, lax.div(a, nz), lax.rem(a, nz))

    sides = [
        (ix > 0, (ix - 1, iy, iz), y_ref.at[0], halo_x.at[1], halo_x.at[0]),
        (ix < nx - 1, (ix + 1, iy, iz), y_ref.at[bx - 1], halo_x.at[0], halo_x.at[1]),
        (line > 0, line_id(line - 1), y_ref.at[:, 0], halo_y.at[1], halo_y.at[0]),
        (line < ny * nz - 1, line_id(line + 1), y_ref.at[:, by - 1], halo_y.at[0], halo_y.at[1]),
    ]

    parts = 4
    px = bx // parts
    loads = [
        pltpu.make_async_copy(y_hbm.at[pl.ds(i * px, px)], y_ref.at[pl.ds(i * px, px)], load_sem.at[i])
        for i in range(parts)
    ]
    for f, src in enumerate((stiff_in, damp_in, dens_in)):
        loads.append(pltpu.make_async_copy(src, fields.at[f], load_sem.at[parts + f]))
    loads.append(pltpu.make_async_copy(ritz_in, ritz_ref, load_sem.at[parts + 3]))
    loads.append(pltpu.make_async_copy(shifts_in, shifts_ref, load_sem.at[parts + 4]))
    for load in loads:
        load.start()

    barrier = pltpu.get_barrier_semaphore()
    def greet(g):
        pl.semaphore_signal(barrier, inc=1, device_id=owners.place(g), device_id_type=MESH)

    def greet_owner(o):
        @pl.when(me != owners.device(o))
        def _():
            greet(owners.device(o))

    def greet_all(g):
        @pl.when(me != g)
        def _():
            greet(g)

    @pl.when(is_owner)
    def _():
        each(devices, greet_all)

    @pl.when(jnp.logical_not(is_owner))
    def _():
        each(count, greet_owner)

    expected = jnp.where(is_owner, devices - 1, count)
    for exists, device, _, _, _ in sides:
        expected = expected + exists.astype(jnp.int32)

        @pl.when(exists)
        def _():
            pl.semaphore_signal(barrier, inc=1, device_id=device, device_id_type=MESH)

    cross = jnp.zeros((2 * w, 2 * w), F32)
    third_order = jnp.zeros((w, w), F32)
    n_rows = px * by * bz
    for i in range(parts):
        loads[i].wait()
        high, mid, low = split3(y_ref[i * px : (i + 1) * px].reshape(n_rows, w))
        two = jnp.concatenate([mid, high], axis=1)
        ys[i * n_rows : (i + 1) * n_rows, : 2 * w] = two
        ys[i * n_rows : (i + 1) * n_rows, 2 * w :] = low
        cross = cross + dot_t(two, two)
        third_order = third_order + dot_t(high, low)
    small = cross[:w, w:] + third_order
    gram = cross[w:, w:] + (cross[:w, :w] + (small + small.T))

    pl.semaphore_wait(barrier, expected)

    def halo_copy(k):
        _, device, src, dst, _ = sides[k]
        other = k ^ 1
        return pltpu.make_async_remote_copy(
            src_ref=src, dst_ref=dst, send_sem=halo_send.at[k], recv_sem=halo_got.at[other],
            device_id=device, device_id_type=MESH,
        )

    def to_owner(slot, o, src, recv, sender):
        return pltpu.make_async_remote_copy(
            src_ref=src.at[o], dst_ref=recv.at[sender], send_sem=a_send.at[slot, o],
            recv_sem=a_got.at[slot, sender], device_id=owners.place(owners.device(o)), device_id_type=MESH,
        )

    def from_owner(slot, g, full, part):
        return pltpu.make_async_remote_copy(
            src_ref=full.at[part], dst_ref=full.at[part], send_sem=b_send.at[slot, g],
            recv_sem=b_got.at[slot, part], device_id=owners.place(g), device_id_type=MESH,
        )

    def each_owner(fn):
        def other(o):
            @pl.when(me != owners.device(o))
            def _():
                fn(o)

        each(count, other)

    def each_device(fn):
        def other(g):
            @pl.when(me != g)
            def _():
                fn(g)

        each(devices, other)

    def reduce_start(slot, mats, src, recv):
        k = len(mats)
        r = mats[0].shape[0] // 2 // count
        for p, mat in enumerate(mats):
            body, ends = pack(mat)
            for o in range(count):
                src[o, p * r : (p + 1) * r, :] = body[o * r : (o + 1) * r]
                src[o, k * r + p : k * r + p + 1, :] = ends
        each_owner(lambda o: to_owner(slot, o, src, recv, me).start())

    def gather_start(slot, src, recv, full):
        @pl.when(is_owner)
        def _():
            recv[me] = src[my_part]
            each_device(lambda g: to_owner(slot, 0, src, recv, g).wait_recv())
            full[my_part] = add_up([recv[g] for g in range(devices)])
            each_device(lambda g: from_owner(slot, g, full, my_part).start())

    def gather_end(slot, full):
        each_owner(lambda o: from_owner(slot, 0, full, o).wait_recv())

    def drain(slot, src, recv, full):
        each_owner(lambda o: to_owner(slot, o, src, recv, me).wait_send())

        @pl.when(is_owner)
        def _():
            each_device(lambda g: from_owner(slot, g, full, my_part).wait_send())

    reduce_start(0, [gram], g_src, g_recv)

    empty = jnp.zeros((bx * by, w - 3 * bz), F32)
    for load in loads[parts:]:
        load.wait()
    cells_ref[...] = jnp.concatenate([fields[0], fields[1], fields[2], empty], axis=1).T
    lanes = bx * by
    shifts = shifts_ref[...].reshape(1, 1, w)
    squares = shifts * shifts

    def spread_step(i, carry):
        cells = pltpu.roll(cells_ref[0 : 3 * bz, :], lax.rem(lanes - i * 2 * by, lanes), 1)
        for dx in range(2):
            k_field = 6.0 + field(cells, 0, dx, by, bz, w)
            c_field = field(cells, 1, dx, by, bz, w)
            m_field = field(cells, 2, dx, by, bz, w)
            spread[0, i * 2 + dx] = k_field
            spread[1, i * 2 + dx] = c_field
            spread[2, i * 2 + dx] = m_field
            diag[i * 2 + dx] = k_field + c_field * shifts + m_field * squares
        return carry

    lax.fori_loop(0, bx // 2, spread_step, 0)

    gather_start(0, g_src, g_recv, g_full)
    gather_end(0, g_full)
    (gram,) = matrices(1, g_full)
    for k, (exists, _, _, _, land) in enumerate(sides):
        @pl.when(exists)
        def _():
            halo_copy(k).start()

        @pl.when(jnp.logical_not(exists))
        def _():
            land[...] = jnp.zeros(land.shape, F32)
    upper, inverse = factorize(gram)
    factor_out[...] = upper / math.sqrt(all_cells)
    tiles = inv_tiles(inverse.T)

    def basis_step(i, total):
        at = pl.multiple_of(i * n_rows, n_rows)
        one = dot(ys[pl.ds(at, n_rows), : 2 * w], tiles[0])
        two = dot(ys[pl.ds(at, n_rows), w:], tiles[1])
        q = (two + one[:, w:]) + one[:, :w]
        pad[pl.ds(i * px + 1, px), 1 : by + 1] = q.reshape(px, by, bz, w)
        high, low = split(q)
        both = jnp.concatenate([high, low], axis=1)
        qs[pl.ds(at, n_rows), :] = both
        return total + dot_t(high, both)

    pair = lax.fori_loop(0, parts, basis_step, jnp.zeros((w, 2 * w), F32))
    small = pair[:, w:]
    reduce_start(1, [pair[:, :w] + (small + small.T)], h_src, h_recv)

    for k, (exists, _, _, _, _) in enumerate(sides):
        @pl.when(exists)
        def _():
            halo_copy(k).wait_send()
            halo_copy(k ^ 1).wait_recv()
    edges = [(pad.at[at, 1 : by + 1], halo_x.at[side]) for side, at in ((0, 0), (1, bx + 1))]
    edges += [(pad.at[1 : bx + 1, at], halo_y.at[side]) for side, at in ((0, 0), (1, by + 1))]
    spots, at = [], 0
    for land, halo in edges:
        size = halo.shape[0] * bz
        q = mm_six(halo[...].reshape(size, w), tiles)
        land[...] = q.reshape(halo.shape)
        hs[at : at + size, :] = jnp.concatenate(split(q), axis=1)
        spots.append((at, size))
        at += size
    for at_x in (0, bx + 1):
        for at_y in (0, by + 1):
            pad[at_x, at_y] = jnp.zeros((bz, w), F32)

    zero = jnp.zeros((by, 1, w), F32)
    proj[...] = jnp.zeros(proj.shape, F32)
    p_rows = 2 * by * bz

    def proj_step(i, carry):
        wides = []
        for dx in range(2):
            q, near = stencil(pad, i * 2 + dx, by, zero)
            k_block = spread[0, i * 2 + dx] * q - near
            c_block = spread[1, i * 2 + dx] * q
            m_block = spread[2, i * 2 + dx] * q + near * (1.0 / 12.0)
            wides.append(jnp.concatenate([v.reshape(by * bz, w) for v in (k_block, c_block, m_block)], axis=1))
        both = qs[pl.ds(pl.multiple_of(i * p_rows, p_rows), p_rows), :]
        qh, ql = both[:, :w], both[:, w:]
        vh, vl = split(jnp.concatenate(wides, axis=0))
        out = dot_t(ql, vh) + dot_t(qh, vl) + dot_t(qh, vh)
        for p in range(3):
            proj[p * w : (p + 1) * w, :] += out[:, p * w : (p + 1) * w]
        return carry

    steps = bx // 2
    cut = steps * 6 // 8
    lax.fori_loop(0, cut, proj_step, 0, unroll=True)
    gather_start(1, h_src, h_recv, h_full)
    lax.fori_loop(cut, steps, proj_step, 0, unroll=True)
    reduce_start(2, [proj[p * w : (p + 1) * w, :] for p in range(3)], p_src, p_recv)
    gather_end(1, h_full)
    (gram,) = matrices(1, h_full)
    _, inverse = factorize(gram, lambda: gather_start(2, p_src, p_recv, p_full))
    inv_out[...] = inverse
    tile = coeff_tile(mm_t_three(inverse, ritz_ref[...]))

    def combine(both):
        out = dot(both, tile)
        return out[:, :w] + out[:, w:]

    for (at, size), (land, halo) in zip(spots, edges):
        land[...] = combine(hs[at : at + size, :]).reshape(halo.shape)
    for i in range(parts):
        v = combine(qs[i * n_rows : (i + 1) * n_rows, :]).reshape(px, by, bz, w)
        pad[i * px + 1 : (i + 1) * px + 1, 1 : by + 1] = v
        vec_out[i * px : (i + 1) * px] = v
    near_scale = squares * (1.0 / 12.0) - 1.0

    def residual_step(i, carry):
        for dx in range(2):
            v, near = stencil(pad, i * 2 + dx, by, zero)
            res_out[i * 2 + dx] = diag[i * 2 + dx] * v + near_scale * near
        return carry

    lax.fori_loop(0, bx // 2, residual_step, 0)
    drain(0, g_src, g_recv, g_full)
    drain(1, h_src, h_recv, h_full)
    gather_end(2, p_full)
    proj_out[...] = p_full[...]
    drain(2, p_src, p_recv, p_full)


def finish(
    vec_in, res_in, proj_in, inv_in, factor_in,
    vec_ref, res_ref, stiff_ref, damp_ref, mass_ref, factor_ref,
    made, sems,
):
    w = factor_ref.shape[0]
    pairs = [(vec_in, vec_ref), (res_in, res_ref), (factor_in, factor_ref)]
    pairs += [(made.at[p], ref) for p, ref in enumerate((stiff_ref, damp_ref, mass_ref))]
    copies = [pltpu.make_async_copy(a, b, sems.at[i]) for i, (a, b) in enumerate(pairs)]
    for copy in copies[:3]:
        copy.start()
    inverse = inv_in[...]
    half = mm(jnp.concatenate(matrices(3, proj_in), axis=0), inverse.T)
    out = mm(inverse, jnp.concatenate([half[p * w : (p + 1) * w] for p in range(3)], axis=1))
    for p in range(3):
        made[p] = out[:, p * w : (p + 1) * w]
        copies[3 + p].start()
    for copy in copies:
        copy.wait()


def local(sizes, moments, stiffness, damping, density, ritz_coeffs, shifts):
    nx, ny, nz, _ = sizes
    bx, by, bz, w = moments.shape
    owners = Owners(nx, ny, nz)
    devices, count = owners.devices, owners.count
    flat = [f.reshape(bx * by, bz) for f in (stiffness, damping, density)]
    r = w // 2 // count + 1
    mat = jax.ShapeDtypeStruct((w, w), F32)
    block = jax.ShapeDtypeStruct(moments.shape, F32)
    square = pltpu.VMEM((w, w), F32)
    hbm = pl.BlockSpec(memory_space=pltpu.HBM)
    vmem = pl.BlockSpec(memory_space=pltpu.VMEM)
    dma = pltpu.SemaphoreType.DMA
    padded = (bx + 2, by + 2, bz, w)

    def stages(rows):
        return [
            pltpu.VMEM((count, rows, w), F32),
            pltpu.VMEM((devices, rows, w), F32),
            pltpu.VMEM((count, rows, w), F32),
        ]

    shared = pl.pallas_call(
        functools.partial(kernel, sizes),
        out_shape=(
            pltpu.VMEM(moments.shape, F32), pltpu.VMEM(moments.shape, F32),
            pltpu.VMEM((count, 3 * r, w), F32), pltpu.VMEM((w, w), F32), pltpu.VMEM((w, w), F32),
        ),
        in_specs=[hbm] * 6,
        out_specs=(vmem,) * 5,
        scratch_shapes=[
            pltpu.VMEM(padded, F32),
            square,
            pltpu.VMEM((3 * w, w), F32),
            pltpu.VMEM(moments.shape, F32),
            pltpu.VMEM((bx * by * bz, 3 * w), BF16),
            pltpu.VMEM((bx * by * bz, 2 * w), BF16),
            pltpu.VMEM((2 * (bx + by) * bz, 2 * w), BF16),
            pltpu.VMEM((3, bx * by, bz), F32),
            pltpu.VMEM((3,) + moments.shape, F32),
            pltpu.VMEM(moments.shape, F32),
            square,
            pltpu.VMEM((1, w), F32),
            pltpu.VMEM((2, by, bz, w), F32),
            pltpu.VMEM((2, bx, bz, w), F32),
            *stages(r), *stages(r), *stages(3 * r),
            dma((9,)),
            dma((4,)), dma((4,)),
            dma((3, count)), dma((3, devices)),
            dma((3, devices)), dma((3, count)),
        ],
        compiler_params=pltpu.CompilerParams(
            collective_id=0, has_side_effects=True, vmem_limit_bytes=32 << 20
        ),
    )(*(pltpu.with_memory_space_constraint(a, pltpu.HBM) for a in (moments, *flat, ritz_coeffs, shifts.reshape(1, w))))
    any_space = pl.BlockSpec(memory_space=pl.ANY)
    return pl.pallas_call(
        finish,
        out_shape=(block, block, mat, mat, mat, mat),
        in_specs=[any_space, any_space, vmem, vmem, any_space],
        out_specs=(hbm,) * 6,
        scratch_shapes=[pltpu.VMEM((3, w, w), F32), dma((6,))],
        compiler_params=pltpu.CompilerParams(vmem_limit_bytes=8 << 20),
    )(*shared)


def solution(mesh):
    nx, ny, nz = (mesh.shape[a] for a in ("gx", "gy", "gz"))

    def call(moments, *rest):
        cells = moments.shape[0] * moments.shape[1] * moments.shape[2]
        body = functools.partial(local, (nx, ny, nz, cells * nx * ny * nz))
        return body(moments, *rest)

    cube = P("gx", ("gy", "gz"), None)
    block = P("gx", ("gy", "gz"), None, None)
    return jax.shard_map(
        call,
        mesh=mesh,
        in_specs=(block, cube, cube, cube, P(), P()),
        out_specs=(block, block, P(), P(), P(), P()),
        check_vma=False,
    )
```

```python
import functools
import math
import jax
import jax.numpy as jnp
from jax import lax
from jax.experimental import pallas as pl
from jax.experimental.pallas import tpu as pltpu
from jax.sharding import PartitionSpec as P

MESH = pl.DeviceIdType.MESH
HI = lax.Precision.HIGHEST
F32 = jnp.float32
BF16 = jnp.bfloat16
BLK = 32
PANEL = 16


def mm(a, b):
    return lax.dot_general(a, b, (((1,), (0,)), ((), ())), precision=HI, preferred_element_type=F32)


def split(x):
    high = x.astype(BF16)
    return high, (x - high.astype(F32)).astype(BF16)


def split3(x):
    high = x.astype(BF16)
    rest = x - high.astype(F32)
    mid = rest.astype(BF16)
    return high, mid, (rest - mid.astype(F32)).astype(BF16)


def dot_t(a, b):
    return lax.dot_general(a, b, (((0,), (0,)), ((), ())), preferred_element_type=F32)


def dot(a, b):
    return lax.dot_general(a, b, (((1,), (0,)), ((), ())), preferred_element_type=F32)


def rank_update(a, b):
    ah, am, al = split3(a)
    bh, bm, bl = split3(b)
    left = jnp.concatenate([ah, am, ah, am, ah, al], axis=0)
    right = jnp.concatenate([bh, bh, bm, bm, bl, bh], axis=0)
    return dot_t(left, right)


def mm_t_three(a, b):
    ah, al = split(a)
    bh, bl = split(b)
    return dot_t(jnp.concatenate([ah, ah, al], axis=0), jnp.concatenate([bh, bl, bh], axis=0))


def coeff_tile(c):
    high, low = split(c)
    return jnp.concatenate(
        [jnp.concatenate([high, low], axis=1), jnp.concatenate([high, jnp.zeros_like(high)], axis=1)], axis=0
    )


def inv_tiles(c):
    high, mid, low = split3(c)
    pair = jnp.concatenate([high, mid], axis=1)
    return jnp.concatenate([pair, pair], axis=0), jnp.concatenate([low, high], axis=0)


def mm_six(rows, tiles):
    w = rows.shape[1]
    high, mid, low = split3(rows)
    one = dot(jnp.concatenate([high, mid], axis=1), tiles[0])
    two = dot(jnp.concatenate([high, low], axis=1), tiles[1])
    return (two + one[:, w:]) + one[:, :w]


def stencil(pad, x, by, zero):
    q = pad[x + 1, 1 : by + 1]
    near = pad[x, 1 : by + 1] + pad[x + 2, 1 : by + 1]
    near = near + pad[x + 1, 0:by] + pad[x + 1, 2 : by + 2]
    near = near + jnp.concatenate([q[:, 1:], zero], axis=1)
    near = near + jnp.concatenate([zero, q[:, :-1]], axis=1)
    return q, near


def field(cells, f, dx, by, bz, w):
    part = cells[f * bz : (f + 1) * bz]
    return jnp.stack([jnp.broadcast_to(part[:, dx * by + y : dx * by + y + 1], (bz, w)) for y in range(by)])


def eliminate(a, first):
    nr, n = a.shape
    lane = lax.broadcasted_iota(jnp.int32, (nr, n), 1)
    row = lax.broadcasted_iota(jnp.int32, (nr, n), 0)
    cols = [jnp.broadcast_to(a[:, first + k : first + k + 1], (nr, n)) for k in range(PANEL)]
    inside = (lane >= first) & (lane < first + PANEL)
    rest = jnp.where(inside, jnp.where(lane == first + row, 1.0, 0.0), a)
    lane, sub = lane[:PANEL], row[:PANEL]
    recips = jnp.zeros((PANEL, n), F32)
    for s in range(PANEL):
        recip = 1.0 / cols[s][s : s + 1]
        recips = jnp.where(sub == s, recip, recips)
        if s == nr - 1:
            break
        m = jnp.where(row > s, cols[s], 0.0) * recip
        for k in range(s + 1, PANEL):
            cols[k] = cols[k] - m * cols[k][s : s + 1]
        rest = rest - m * rest[s : s + 1]
    done = rest[:PANEL]
    e = jnp.where(lane < first + PANEL, done, 0.0)
    u = jnp.where(lane >= first + PANEL, done, 0.0)
    for k in range(PANEL):
        u = jnp.where((lane == first + k) & (sub <= k), cols[k][:PANEL], u)
    return u, e, recips, rest[PANEL:]


def factorize(g, between=None):
    n = g.shape[0]
    blocks = n // BLK
    rows = [g[b * BLK : (b + 1) * BLK] for b in range(blocks)]
    upper, inverse = [], []
    lane = lax.broadcasted_iota(jnp.int32, (BLK, n), 1)
    for j in range(blocks):
        first = j * BLK
        a = rows[j]
        parts = []
        for p in range(BLK // PANEL):
            u, e, recips, a = eliminate(a, first + p * PANEL)
            parts.append((u, e, recips))
        u, e, recips = (jnp.concatenate(x, axis=0) for x in zip(*parts))
        if j < blocks - 1:
            beyond = jnp.where(lane >= first + BLK, u, 0.0)
            update = rank_update(beyond * recips, beyond + e)
            inside = (lane >= first) & (lane < first + BLK)
            for b in range(j + 1, blocks):
                rows[b] = jnp.where(inside, 0.0, rows[b]) - update[b * BLK : (b + 1) * BLK]
        scale = jnp.sqrt(recips)
        upper.append(u * scale)
        inverse.append(e * scale)
        if between and j == 0:
            between()
    return jnp.concatenate(upper, axis=0), jnp.concatenate(inverse, axis=0)


def halves(h, w):
    row = lax.broadcasted_iota(jnp.int32, (h, w), 0)
    lane = lax.broadcasted_iota(jnp.int32, (h, w), 1)
    return row, lane


def pack(g):
    w = g.shape[0]
    h = w // 2
    row, lane = halves(h, w)
    top, low = g[:h], g[h:]
    turned = pltpu.roll(low, h, 1)
    body = jnp.where((lane >= h) | (row >= lane), top, turned)
    ends = jnp.where(row == lane, turned, 0.0) + jnp.where(row == lane - h, low, 0.0)
    return body, jnp.sum(ends, axis=0, keepdims=True)


def unpack(body, ends):
    h, w = body.shape
    row, lane = halves(h, w)
    flipped = jnp.concatenate([body, body], axis=0).T
    top = jnp.where((lane >= h) | (row >= lane), body, flipped[:h])
    last = jnp.where(row == lane - h, jnp.broadcast_to(ends, (h, w)), flipped[:h])
    last = jnp.where(row < lane - h, pltpu.roll(body, h, 1), last)
    return jnp.concatenate([top, jnp.where(lane < h, flipped[h:], last)], axis=0)


def matrices(k, full):
    count = full.shape[0]
    r = full.shape[1] // k - 1
    out = []
    for p in range(k):
        body = jnp.concatenate([full[o, p * r : (p + 1) * r, :] for o in range(count)], axis=0)
        out.append(unpack(body, full[0, k * r + p : k * r + p + 1, :]))
    return out


def each(n, fn):
    if n <= 64:
        for g in range(n):
            fn(g)
    else:
        def step(g, carry):
            fn(g)
            return carry

        lax.fori_loop(0, n, step, 0)


def add_up(terms):
    while len(terms) > 1:
        pairs = [terms[i] + terms[i + 1] for i in range(0, len(terms) - 1, 2)]
        terms = pairs + terms[len(pairs) * 2 :]
    return terms[0]


class Owners:
    def __init__(self, nx, ny, nz):
        self.stride = 2 if nz % 2 == 0 else 1
        self.span = 2 if ny % 2 == 0 else 1
        self.first = (ny - self.span) // 2
        self.nz, self.group = nz, nx * nz
        self.in_plane = self.group // self.stride
        self.count = self.span * self.in_plane
        self.devices = self.group * ny

    def holds(self, iy, iz):
        middle = (iy >= self.first) & (iy < self.first + self.span)
        return middle & (lax.rem(iz, self.stride) == self.stride - 1)

    def part(self, iy, mine):
        return (iy - self.first) * self.in_plane + lax.div(mine, self.stride)

    def device(self, o):
        plane = self.first + o // self.in_plane
        return plane * self.group + o % self.in_plane * self.stride + self.stride - 1

    def place(self, g):
        a = g % self.group
        return (a // self.nz, g // self.group, a % self.nz)


def kernel(
    sizes,
    y_hbm, stiff_in, damp_in, dens_in, ritz_in, shifts_in,
    vec_out, res_out, proj_out, inv_out, factor_out,
    pad, cells_ref, proj,
    y_ref, ys, qs, hs, fields, spread, diag, ritz_ref, shifts_ref, halo_x, halo_y,
    g_src, g_recv, g_full, h_src, h_recv, h_full, p_src, p_recv, p_full, load_sem,
    halo_send, halo_got, a_send, a_got, b_send, b_got,
):
    nx, ny, nz, all_cells = sizes
    bx, by, bz, w = y_ref.shape
    ix, iy, iz = lax.axis_index("gx"), lax.axis_index("gy"), lax.axis_index("gz")
    owners = Owners(nx, ny, nz)
    devices, count = owners.devices, owners.count
    mine = ix * nz + iz
    me = iy * owners.group + mine
    line = iy * nz + iz
    is_owner = owners.holds(iy, iz)
    my_part = owners.part(iy, mine)

    def line_id(a):
        return (ix, lax.div(a, nz), lax.rem(a, nz))

    sides = [
        (ix > 0, (ix - 1, iy, iz), y_ref.at[0], halo_x.at[1], halo_x.at[0]),
        (ix < nx - 1, (ix + 1, iy, iz), y_ref.at[bx - 1], halo_x.at[0], halo_x.at[1]),
        (line > 0, line_id(line - 1), y_ref.at[:, 0], halo_y.at[1], halo_y.at[0]),
        (line < ny * nz - 1, line_id(line + 1), y_ref.at[:, by - 1], halo_y.at[0], halo_y.at[1]),
    ]

    parts = 4
    px = bx // parts
    loads = [
        pltpu.make_async_copy(y_hbm.at[pl.ds(i * px, px)], y_ref.at[pl.ds(i * px, px)], load_sem.at[i])
        for i in range(parts)
    ]
    for f, src in enumerate((stiff_in, damp_in, dens_in)):
        loads.append(pltpu.make_async_copy(src, fields.at[f], load_sem.at[parts + f]))
    loads.append(pltpu.make_async_copy(ritz_in, ritz_ref, load_sem.at[parts + 3]))
    loads.append(pltpu.make_async_copy(shifts_in, shifts_ref, load_sem.at[parts + 4]))
    for load in loads:
        load.start()

    barrier = pltpu.get_barrier_semaphore()
    def greet(g):
        pl.semaphore_signal(barrier, inc=1, device_id=owners.place(g), device_id_type=MESH)

    def greet_owner(o):
        @pl.when(me != owners.device(o))
        def _():
            greet(owners.device(o))

    def greet_all(g):
        @pl.when(me != g)
        def _():
            greet(g)

    @pl.when(is_owner)
    def _():
        each(devices, greet_all)

    @pl.when(jnp.logical_not(is_owner))
    def _():
        each(count, greet_owner)

    expected = jnp.where(is_owner, devices - 1, count)
    for exists, device, _, _, _ in sides:
        expected = expected + exists.astype(jnp.int32)

        @pl.when(exists)
        def _():
            pl.semaphore_signal(barrier, inc=1, device_id=device, device_id_type=MESH)

    cross = jnp.zeros((2 * w, 2 * w), F32)
    third_order = jnp.zeros((w, w), F32)
    n_rows = px * by * bz
    for i in range(parts):
        loads[i].wait()
        high, mid, low = split3(y_ref[i * px : (i + 1) * px].reshape(n_rows, w))
        two = jnp.concatenate([mid, high], axis=1)
        ys[i * n_rows : (i + 1) * n_rows, : 2 * w] = two
        ys[i * n_rows : (i + 1) * n_rows, 2 * w :] = low
        cross = cross + dot_t(two, two)
        third_order = third_order + dot_t(high, low)
    small = cross[:w, w:] + third_order
    gram = cross[w:, w:] + (cross[:w, :w] + (small + small.T))

    pl.semaphore_wait(barrier, expected)

    def halo_copy(k):
        _, device, src, dst, _ = sides[k]
        other = k ^ 1
        return pltpu.make_async_remote_copy(
            src_ref=src, dst_ref=dst, send_sem=halo_send.at[k], recv_sem=halo_got.at[other],
            device_id=device, device_id_type=MESH,
        )

    def to_owner(slot, o, src, recv, sender):
        return pltpu.make_async_remote_copy(
            src_ref=src.at[o], dst_ref=recv.at[sender], send_sem=a_send.at[slot, o],
            recv_sem=a_got.at[slot, sender], device_id=owners.place(owners.device(o)), device_id_type=MESH,
        )

    def from_owner(slot, g, full, part):
        return pltpu.make_async_remote_copy(
            src_ref=full.at[part], dst_ref=full.at[part], send_sem=b_send.at[slot, g],
            recv_sem=b_got.at[slot, part], device_id=owners.place(g), device_id_type=MESH,
        )

    def each_owner(fn):
        def other(o):
            @pl.when(me != owners.device(o))
            def _():
                fn(o)

        each(count, other)

    def each_device(fn):
        def other(g):
            @pl.when(me != g)
            def _():
                fn(g)

        each(devices, other)

    def reduce_start(slot, mats, src, recv):
        k = len(mats)
        r = mats[0].shape[0] // 2 // count
        for p, mat in enumerate(mats):
            body, ends = pack(mat)
            for o in range(count):
                src[o, p * r : (p + 1) * r, :] = body[o * r : (o + 1) * r]
                src[o, k * r + p : k * r + p + 1, :] = ends
        each_owner(lambda o: to_owner(slot, o, src, recv, me).start())

    def gather_start(slot, src, recv, full):
        @pl.when(is_owner)
        def _():
            recv[me] = src[my_part]
            each_device(lambda g: to_owner(slot, 0, src, recv, g).wait_recv())
            full[my_part] = add_up([recv[g] for g in range(devices)])
            each_device(lambda g: from_owner(slot, g, full, my_part).start())

    def gather_end(slot, full):
        each_owner(lambda o: from_owner(slot, 0, full, o).wait_recv())

    def drain(slot, src, recv, full):
        each_owner(lambda o: to_owner(slot, o, src, recv, me).wait_send())

        @pl.when(is_owner)
        def _():
            each_device(lambda g: from_owner(slot, g, full, my_part).wait_send())

    reduce_start(0, [gram], g_src, g_recv)

    empty = jnp.zeros((bx * by, w - 3 * bz), F32)
    for load in loads[parts:]:
        load.wait()
    cells_ref[...] = jnp.concatenate([fields[0], fields[1], fields[2], empty], axis=1).T
    lanes = bx * by
    shifts = shifts_ref[...].reshape(1, 1, w)
    squares = shifts * shifts

    def spread_step(i, carry):
        cells = pltpu.roll(cells_ref[0 : 3 * bz, :], lax.rem(lanes - i * 2 * by, lanes), 1)
        for dx in range(2):
            k_field = 6.0 + field(cells, 0, dx, by, bz, w)
            c_field = field(cells, 1, dx, by, bz, w)
            m_field = field(cells, 2, dx, by, bz, w)
            spread[0, i * 2 + dx] = k_field
            spread[1, i * 2 + dx] = c_field
            spread[2, i * 2 + dx] = m_field
            diag[i * 2 + dx] = k_field + c_field * shifts + m_field * squares
        return carry

    lax.fori_loop(0, bx // 2, spread_step, 0)

    gather_start(0, g_src, g_recv, g_full)
    gather_end(0, g_full)
    (gram,) = matrices(1, g_full)
    for k, (exists, _, _, _, land) in enumerate(sides):
        @pl.when(exists)
        def _():
            halo_copy(k).start()

        @pl.when(jnp.logical_not(exists))
        def _():
            land[...] = jnp.zeros(land.shape, F32)
    upper, inverse = factorize(gram)
    factor_out[...] = upper / math.sqrt(all_cells)
    tiles = inv_tiles(inverse.T)

    def basis_step(i, total):
        at = pl.multiple_of(i * n_rows, n_rows)
        one = dot(ys[pl.ds(at, n_rows), : 2 * w], tiles[0])
        two = dot(ys[pl.ds(at, n_rows), w:], tiles[1])
        q = (two + one[:, w:]) + one[:, :w]
        pad[pl.ds(i * px + 1, px), 1 : by + 1] = q.reshape(px, by, bz, w)
        high, low = split(q)
        both = jnp.concatenate([high, low], axis=1)
        qs[pl.ds(at, n_rows), :] = both
        return total + dot_t(high, both)

    pair = lax.fori_loop(0, parts, basis_step, jnp.zeros((w, 2 * w), F32), unroll=True)
    small = pair[:, w:]
    reduce_start(1, [pair[:, :w] + (small + small.T)], h_src, h_recv)

    for k, (exists, _, _, _, _) in enumerate(sides):
        @pl.when(exists)
        def _():
            halo_copy(k).wait_send()
            halo_copy(k ^ 1).wait_recv()
    edges = [(pad.at[at, 1 : by + 1], halo_x.at[side]) for side, at in ((0, 0), (1, bx + 1))]
    edges += [(pad.at[1 : bx + 1, at], halo_y.at[side]) for side, at in ((0, 0), (1, by + 1))]
    spots, at = [], 0
    for land, halo in edges:
        size = halo.shape[0] * bz
        q = mm_six(halo[...].reshape(size, w), tiles)
        land[...] = q.reshape(halo.shape)
        hs[at : at + size, :] = jnp.concatenate(split(q), axis=1)
        spots.append((at, size))
        at += size
    for at_x in (0, bx + 1):
        for at_y in (0, by + 1):
            pad[at_x, at_y] = jnp.zeros((bz, w), F32)

    zero = jnp.zeros((by, 1, w), F32)
    proj[...] = jnp.zeros(proj.shape, F32)
    p_rows = 2 * by * bz

    def proj_step(i, carry):
        wides = []
        for dx in range(2):
            q, near = stencil(pad, i * 2 + dx, by, zero)
            k_block = spread[0, i * 2 + dx] * q - near
            c_block = spread[1, i * 2 + dx] * q
            m_block = spread[2, i * 2 + dx] * q + near * (1.0 / 12.0)
            wides.append(jnp.concatenate([v.reshape(by * bz, w) for v in (k_block, c_block, m_block)], axis=1))
        both = qs[pl.ds(pl.multiple_of(i * p_rows, p_rows), p_rows), :]
        qh, ql = both[:, :w], both[:, w:]
        vh, vl = split(jnp.concatenate(wides, axis=0))
        out = dot_t(ql, vh) + dot_t(qh, vl) + dot_t(qh, vh)
        for p in range(3):
            proj[p * w : (p + 1) * w, :] += out[:, p * w : (p + 1) * w]
        return carry

    steps = bx // 2
    cut = steps * 6 // 8
    lax.fori_loop(0, cut, proj_step, 0, unroll=True)
    gather_start(1, h_src, h_recv, h_full)
    lax.fori_loop(cut, steps, proj_step, 0, unroll=True)
    reduce_start(2, [proj[p * w : (p + 1) * w, :] for p in range(3)], p_src, p_recv)
    gather_end(1, h_full)
    (gram,) = matrices(1, h_full)
    _, inverse = factorize(gram, lambda: gather_start(2, p_src, p_recv, p_full))
    inv_out[...] = inverse
    tile = coeff_tile(mm_t_three(inverse, ritz_ref[...]))

    def combine(both):
        out = dot(both, tile)
        return out[:, :w] + out[:, w:]

    for (at, size), (land, halo) in zip(spots, edges):
        land[...] = combine(hs[at : at + size, :]).reshape(halo.shape)
    for i in range(parts):
        v = combine(qs[i * n_rows : (i + 1) * n_rows, :]).reshape(px, by, bz, w)
        pad[i * px + 1 : (i + 1) * px + 1, 1 : by + 1] = v
        vec_out[i * px : (i + 1) * px] = v
    near_scale = squares * (1.0 / 12.0) - 1.0

    def residual_step(i, carry):
        for dx in range(2):
            v, near = stencil(pad, i * 2 + dx, by, zero)
            res_out[i * 2 + dx] = diag[i * 2 + dx] * v + near_scale * near
        return carry

    lax.fori_loop(0, bx // 2, residual_step, 0)
    drain(0, g_src, g_recv, g_full)
    drain(1, h_src, h_recv, h_full)
    gather_end(2, p_full)
    proj_out[...] = p_full[...]
    drain(2, p_src, p_recv, p_full)


def finish(
    vec_in, res_in, proj_in, inv_in, factor_in,
    vec_ref, res_ref, stiff_ref, damp_ref, mass_ref, factor_ref,
    made, sems,
):
    w = factor_ref.shape[0]
    pairs = [(vec_in, vec_ref), (res_in, res_ref), (factor_in, factor_ref)]
    pairs += [(made.at[p], ref) for p, ref in enumerate((stiff_ref, damp_ref, mass_ref))]
    copies = [pltpu.make_async_copy(a, b, sems.at[i]) for i, (a, b) in enumerate(pairs)]
    for copy in copies[:3]:
        copy.start()
    inverse = inv_in[...]
    half = mm(jnp.concatenate(matrices(3, proj_in), axis=0), inverse.T)
    out = mm(inverse, jnp.concatenate([half[p * w : (p + 1) * w] for p in range(3)], axis=1))
    for p in range(3):
        made[p] = out[:, p * w : (p + 1) * w]
        copies[3 + p].start()
    for copy in copies:
        copy.wait()


def local(sizes, moments, stiffness, damping, density, ritz_coeffs, shifts):
    nx, ny, nz, _ = sizes
    bx, by, bz, w = moments.shape
    owners = Owners(nx, ny, nz)
    devices, count = owners.devices, owners.count
    flat = [f.reshape(bx * by, bz) for f in (stiffness, damping, density)]
    r = w // 2 // count + 1
    mat = jax.ShapeDtypeStruct((w, w), F32)
    block = jax.ShapeDtypeStruct(moments.shape, F32)
    square = pltpu.VMEM((w, w), F32)
    hbm = pl.BlockSpec(memory_space=pltpu.HBM)
    vmem = pl.BlockSpec(memory_space=pltpu.VMEM)
    dma = pltpu.SemaphoreType.DMA
    padded = (bx + 2, by + 2, bz, w)

    def stages(rows):
        return [
            pltpu.VMEM((count, rows, w), F32),
            pltpu.VMEM((devices, rows, w), F32),
            pltpu.VMEM((count, rows, w), F32),
        ]

    shared = pl.pallas_call(
        functools.partial(kernel, sizes),
        out_shape=(
            pltpu.VMEM(moments.shape, F32), pltpu.VMEM(moments.shape, F32),
            pltpu.VMEM((count, 3 * r, w), F32), pltpu.VMEM((w, w), F32), pltpu.VMEM((w, w), F32),
        ),
        in_specs=[hbm] * 6,
        out_specs=(vmem,) * 5,
        scratch_shapes=[
            pltpu.VMEM(padded, F32),
            square,
            pltpu.VMEM((3 * w, w), F32),
            pltpu.VMEM(moments.shape, F32),
            pltpu.VMEM((bx * by * bz, 3 * w), BF16),
            pltpu.VMEM((bx * by * bz, 2 * w), BF16),
            pltpu.VMEM((2 * (bx + by) * bz, 2 * w), BF16),
            pltpu.VMEM((3, bx * by, bz), F32),
            pltpu.VMEM((3,) + moments.shape, F32),
            pltpu.VMEM(moments.shape, F32),
            square,
            pltpu.VMEM((1, w), F32),
            pltpu.VMEM((2, by, bz, w), F32),
            pltpu.VMEM((2, bx, bz, w), F32),
            *stages(r), *stages(r), *stages(3 * r),
            dma((9,)),
            dma((4,)), dma((4,)),
            dma((3, count)), dma((3, devices)),
            dma((3, devices)), dma((3, count)),
        ],
        compiler_params=pltpu.CompilerParams(
            collective_id=0, has_side_effects=True, vmem_limit_bytes=32 << 20
        ),
    )(*(pltpu.with_memory_space_constraint(a, pltpu.HBM) for a in (moments, *flat, ritz_coeffs, shifts.reshape(1, w))))
    any_space = pl.BlockSpec(memory_space=pl.ANY)
    return pl.pallas_call(
        finish,
        out_shape=(block, block, mat, mat, mat, mat),
        in_specs=[any_space, any_space, vmem, vmem, any_space],
        out_specs=(hbm,) * 6,
        scratch_shapes=[pltpu.VMEM((3, w, w), F32), dma((6,))],
        compiler_params=pltpu.CompilerParams(vmem_limit_bytes=8 << 20),
    )(*shared)


def solution(mesh):
    nx, ny, nz = (mesh.shape[a] for a in ("gx", "gy", "gz"))

    def call(moments, *rest):
        cells = moments.shape[0] * moments.shape[1] * moments.shape[2]
        body = functools.partial(local, (nx, ny, nz, cells * nx * ny * nz))
        return body(moments, *rest)

    cube = P("gx", ("gy", "gz"), None)
    block = P("gx", ("gy", "gz"), None, None)
    return jax.shard_map(
        call,
        mesh=mesh,
        in_specs=(block, cube, cube, cube, P(), P()),
        out_specs=(block, block, P(), P(), P(), P()),
        check_vma=False,
    )
```

```python
import functools
import math
import jax
import jax.numpy as jnp
from jax import lax
from jax.experimental import pallas as pl
from jax.experimental.pallas import tpu as pltpu
from jax.sharding import PartitionSpec as P

MESH = pl.DeviceIdType.MESH
HI = lax.Precision.HIGHEST
F32 = jnp.float32
BF16 = jnp.bfloat16
BLK = 32
PANEL = 16


def mm(a, b):
    return lax.dot_general(a, b, (((1,), (0,)), ((), ())), precision=HI, preferred_element_type=F32)


def split(x):
    high = x.astype(BF16)
    return high, (x - high.astype(F32)).astype(BF16)


def split3(x):
    high = x.astype(BF16)
    rest = x - high.astype(F32)
    mid = rest.astype(BF16)
    return high, mid, (rest - mid.astype(F32)).astype(BF16)


def dot_t(a, b):
    return lax.dot_general(a, b, (((0,), (0,)), ((), ())), preferred_element_type=F32)


def dot(a, b):
    return lax.dot_general(a, b, (((1,), (0,)), ((), ())), preferred_element_type=F32)


def rank_update(a, b):
    ah, am, al = split3(a)
    bh, bm, bl = split3(b)
    left = jnp.concatenate([ah, am, ah, am, ah, al], axis=0)
    right = jnp.concatenate([bh, bh, bm, bm, bl, bh], axis=0)
    return dot_t(left, right)


def mm_t_three(a, b):
    ah, al = split(a)
    bh, bl = split(b)
    return dot_t(jnp.concatenate([ah, ah, al], axis=0), jnp.concatenate([bh, bl, bh], axis=0))


def coeff_tile(c):
    high, low = split(c)
    return jnp.concatenate(
        [jnp.concatenate([high, low], axis=1), jnp.concatenate([high, jnp.zeros_like(high)], axis=1)], axis=0
    )


def inv_tiles(c):
    high, mid, low = split3(c)
    pair = jnp.concatenate([high, mid], axis=1)
    return jnp.concatenate([pair, pair], axis=0), jnp.concatenate([low, high], axis=0)


def mm_six(rows, tiles):
    w = rows.shape[1]
    high, mid, low = split3(rows)
    one = dot(jnp.concatenate([high, mid], axis=1), tiles[0])
    two = dot(jnp.concatenate([high, low], axis=1), tiles[1])
    return (two + one[:, w:]) + one[:, :w]


def stencil(pad, x, by, zero):
    q = pad[x + 1, 1 : by + 1]
    near = pad[x, 1 : by + 1] + pad[x + 2, 1 : by + 1]
    near = near + pad[x + 1, 0:by] + pad[x + 1, 2 : by + 2]
    near = near + jnp.concatenate([q[:, 1:], zero], axis=1)
    near = near + jnp.concatenate([zero, q[:, :-1]], axis=1)
    return q, near


def field(cells, f, dx, by, bz, w):
    part = cells[f * bz : (f + 1) * bz]
    return jnp.stack([jnp.broadcast_to(part[:, dx * by + y : dx * by + y + 1], (bz, w)) for y in range(by)])


def eliminate(a, first):
    nr, n = a.shape
    lane = lax.broadcasted_iota(jnp.int32, (nr, n), 1)
    row = lax.broadcasted_iota(jnp.int32, (nr, n), 0)
    cols = [jnp.broadcast_to(a[:, first + k : first + k + 1], (nr, n)) for k in range(PANEL)]
    inside = (lane >= first) & (lane < first + PANEL)
    rest = jnp.where(inside, jnp.where(lane == first + row, 1.0, 0.0), a)
    lane, sub = lane[:PANEL], row[:PANEL]
    recips = jnp.zeros((PANEL, n), F32)
    for s in range(PANEL):
        recip = 1.0 / cols[s][s : s + 1]
        recips = jnp.where(sub == s, recip, recips)
        if s == nr - 1:
            break
        m = jnp.where(row > s, cols[s], 0.0) * recip
        for k in range(s + 1, PANEL):
            cols[k] = cols[k] - m * cols[k][s : s + 1]
        rest = rest - m * rest[s : s + 1]
    done = rest[:PANEL]
    e = jnp.where(lane < first + PANEL, done, 0.0)
    u = jnp.where(lane >= first + PANEL, done, 0.0)
    for k in range(PANEL):
        u = jnp.where((lane == first + k) & (sub <= k), cols[k][:PANEL], u)
    return u, e, recips, rest[PANEL:]


def factorize(g, between=None):
    n = g.shape[0]
    blocks = n // BLK
    rows = [g[b * BLK : (b + 1) * BLK] for b in range(blocks)]
    upper, inverse = [], []
    lane = lax.broadcasted_iota(jnp.int32, (BLK, n), 1)
    for j in range(blocks):
        first = j * BLK
        a = rows[j]
        parts = []
        for p in range(BLK // PANEL):
            u, e, recips, a = eliminate(a, first + p * PANEL)
            parts.append((u, e, recips))
        u, e, recips = (jnp.concatenate(x, axis=0) for x in zip(*parts))
        if j < blocks - 1:
            beyond = jnp.where(lane >= first + BLK, u, 0.0)
            update = rank_update(beyond * recips, beyond + e)
            inside = (lane >= first) & (lane < first + BLK)
            for b in range(j + 1, blocks):
                rows[b] = jnp.where(inside, 0.0, rows[b]) - update[b * BLK : (b + 1) * BLK]
        scale = jnp.sqrt(recips)
        upper.append(u * scale)
        inverse.append(e * scale)
        if between and j == 0:
            between()
    return jnp.concatenate(upper, axis=0), jnp.concatenate(inverse, axis=0)


def halves(h, w):
    row = lax.broadcasted_iota(jnp.int32, (h, w), 0)
    lane = lax.broadcasted_iota(jnp.int32, (h, w), 1)
    return row, lane


def pack(g):
    w = g.shape[0]
    h = w // 2
    row, lane = halves(h, w)
    top, low = g[:h], g[h:]
    turned = pltpu.roll(low, h, 1)
    body = jnp.where((lane >= h) | (row >= lane), top, turned)
    ends = jnp.where(row == lane, turned, 0.0) + jnp.where(row == lane - h, low, 0.0)
    return body, jnp.sum(ends, axis=0, keepdims=True)


def unpack(body, ends):
    h, w = body.shape
    row, lane = halves(h, w)
    flipped = jnp.concatenate([body, body], axis=0).T
    top = jnp.where((lane >= h) | (row >= lane), body, flipped[:h])
    last = jnp.where(row == lane - h, jnp.broadcast_to(ends, (h, w)), flipped[:h])
    last = jnp.where(row < lane - h, pltpu.roll(body, h, 1), last)
    return jnp.concatenate([top, jnp.where(lane < h, flipped[h:], last)], axis=0)


def matrices(k, full):
    count = full.shape[0]
    r = full.shape[1] // k - 1
    out = []
    for p in range(k):
        body = jnp.concatenate([full[o, p * r : (p + 1) * r, :] for o in range(count)], axis=0)
        out.append(unpack(body[: body.shape[1] // 2], full[0, k * r + p : k * r + p + 1, :]))
    return out


def each(n, fn):
    if n <= 64:
        for g in range(n):
            fn(g)
    else:
        def step(g, carry):
            fn(g)
            return carry

        lax.fori_loop(0, n, step, 0)


def add_up(terms):
    while len(terms) > 1:
        pairs = [terms[i] + terms[i + 1] for i in range(0, len(terms) - 1, 2)]
        terms = pairs + terms[len(pairs) * 2 :]
    return terms[0]


class Owners:
    def __init__(self, nx, ny, nz):
        stride = 2 if nz % 2 == 0 else 1
        span = 2 if ny % 2 == 0 else 1
        first = (ny - span) // 2
        self.nz, self.group = nz, nx * nz
        self.devices = self.group * ny
        table = [
            plane * self.group + a
            for plane in range(first, first + span)
            for a in range(stride - 1, self.group, stride)
        ]
        self.table = table[1:-1] if len(table) > 4 else table
        self.count = len(self.table)

    def holds(self, me):
        held = me == self.table[0]
        for g in self.table[1:]:
            held = held | (me == g)
        return held

    def part(self, me):
        part = jnp.int32(0)
        for o, g in enumerate(self.table):
            part = part + jnp.where(me == g, o, 0)
        return part

    def device(self, o):
        return self.table[o]

    def place(self, g):
        a = g % self.group
        return (a // self.nz, g // self.group, a % self.nz)


def kernel(
    sizes,
    y_hbm, stiff_in, damp_in, dens_in, ritz_in, shifts_in,
    vec_out, res_out, proj_out, inv_out, factor_out,
    pad, cells_ref, proj,
    y_ref, ys, qs, hs, fields, spread, diag, ritz_ref, shifts_ref, halo_x, halo_y,
    g_src, g_recv, g_full, h_src, h_recv, h_full, p_src, p_recv, p_full, load_sem,
    halo_send, halo_got, a_send, a_got, b_send, b_got,
):
    nx, ny, nz, all_cells = sizes
    bx, by, bz, w = y_ref.shape
    ix, iy, iz = lax.axis_index("gx"), lax.axis_index("gy"), lax.axis_index("gz")
    owners = Owners(nx, ny, nz)
    devices, count = owners.devices, owners.count
    mine = ix * nz + iz
    me = iy * owners.group + mine
    line = iy * nz + iz
    is_owner = owners.holds(me)
    my_part = owners.part(me)

    def line_id(a):
        return (ix, lax.div(a, nz), lax.rem(a, nz))

    sides = [
        (ix > 0, (ix - 1, iy, iz), y_ref.at[0], halo_x.at[1], halo_x.at[0]),
        (ix < nx - 1, (ix + 1, iy, iz), y_ref.at[bx - 1], halo_x.at[0], halo_x.at[1]),
        (line > 0, line_id(line - 1), y_ref.at[:, 0], halo_y.at[1], halo_y.at[0]),
        (line < ny * nz - 1, line_id(line + 1), y_ref.at[:, by - 1], halo_y.at[0], halo_y.at[1]),
    ]

    parts = 2
    px = bx // parts
    loads = [
        pltpu.make_async_copy(y_hbm.at[pl.ds(i * px, px)], y_ref.at[pl.ds(i * px, px)], load_sem.at[i])
        for i in range(parts)
    ]
    for f, src in enumerate((stiff_in, damp_in, dens_in)):
        loads.append(pltpu.make_async_copy(src, fields.at[f], load_sem.at[parts + f]))
    loads.append(pltpu.make_async_copy(ritz_in, ritz_ref, load_sem.at[parts + 3]))
    loads.append(pltpu.make_async_copy(shifts_in, shifts_ref, load_sem.at[parts + 4]))
    for load in loads:
        load.start()

    barrier = pltpu.get_barrier_semaphore()
    def greet(g):
        pl.semaphore_signal(barrier, inc=1, device_id=owners.place(g), device_id_type=MESH)

    def greet_owner(o):
        @pl.when(me != owners.device(o))
        def _():
            greet(owners.device(o))

    def greet_all(g):
        @pl.when(me != g)
        def _():
            greet(g)

    @pl.when(is_owner)
    def _():
        each(devices, greet_all)

    @pl.when(jnp.logical_not(is_owner))
    def _():
        each(count, greet_owner)

    expected = jnp.where(is_owner, devices - 1, count)
    for exists, device, _, _, _ in sides:
        expected = expected + exists.astype(jnp.int32)

        @pl.when(exists)
        def _():
            pl.semaphore_signal(barrier, inc=1, device_id=device, device_id_type=MESH)

    cross = jnp.zeros((2 * w, 2 * w), F32)
    third_order = jnp.zeros((w, w), F32)
    n_rows = px * by * bz
    for i in range(parts):
        loads[i].wait()
        high, mid, low = split3(y_ref[i * px : (i + 1) * px].reshape(n_rows, w))
        two = jnp.concatenate([mid, high], axis=1)
        ys[i * n_rows : (i + 1) * n_rows, : 2 * w] = two
        ys[i * n_rows : (i + 1) * n_rows, 2 * w :] = low
        cross = cross + dot_t(two, two)
        third_order = third_order + dot_t(high, low)
    small = cross[:w, w:] + third_order
    gram = cross[w:, w:] + (cross[:w, :w] + (small + small.T))

    pl.semaphore_wait(barrier, expected)

    def halo_copy(k):
        _, device, src, dst, _ = sides[k]
        other = k ^ 1
        return pltpu.make_async_remote_copy(
            src_ref=src, dst_ref=dst, send_sem=halo_send.at[k], recv_sem=halo_got.at[other],
            device_id=device, device_id_type=MESH,
        )

    def to_owner(slot, o, src, recv, sender):
        return pltpu.make_async_remote_copy(
            src_ref=src.at[o], dst_ref=recv.at[sender], send_sem=a_send.at[slot, o],
            recv_sem=a_got.at[slot, sender], device_id=owners.place(owners.device(o)), device_id_type=MESH,
        )

    def from_owner(slot, g, full, part):
        return pltpu.make_async_remote_copy(
            src_ref=full.at[part], dst_ref=full.at[part], send_sem=b_send.at[slot, g],
            recv_sem=b_got.at[slot, part], device_id=owners.place(g), device_id_type=MESH,
        )

    def each_owner(fn):
        def other(o):
            @pl.when(me != owners.device(o))
            def _():
                fn(o)

        each(count, other)

    def each_device(fn):
        def other(g):
            @pl.when(me != g)
            def _():
                fn(g)

        each(devices, other)

    def reduce_start(slot, mats, src, recv):
        k = len(mats)
        r = src.shape[1] // k - 1
        for p, mat in enumerate(mats):
            body, ends = pack(mat)
            spare = r * count - body.shape[0]
            if spare:
                body = jnp.concatenate([body, jnp.zeros((spare, w), F32)], axis=0)
            for o in range(count):
                src[o, p * r : (p + 1) * r, :] = body[o * r : (o + 1) * r]
                src[o, k * r + p : k * r + p + 1, :] = ends
        each_owner(lambda o: to_owner(slot, o, src, recv, me).start())

    def gather_start(slot, src, recv, full):
        @pl.when(is_owner)
        def _():
            recv[me] = src[my_part]
            each_device(lambda g: to_owner(slot, 0, src, recv, g).wait_recv())
            full[my_part] = add_up([recv[g] for g in range(devices)])
            each_device(lambda g: from_owner(slot, g, full, my_part).start())

    def gather_end(slot, full):
        each_owner(lambda o: from_owner(slot, 0, full, o).wait_recv())

    def drain(slot, src, recv, full):
        each_owner(lambda o: to_owner(slot, o, src, recv, me).wait_send())

        @pl.when(is_owner)
        def _():
            each_device(lambda g: from_owner(slot, g, full, my_part).wait_send())

    reduce_start(0, [gram], g_src, g_recv)

    empty = jnp.zeros((bx * by, w - 3 * bz), F32)
    for load in loads[parts:]:
        load.wait()
    cells_ref[...] = jnp.concatenate([fields[0], fields[1], fields[2], empty], axis=1).T
    lanes = bx * by
    shifts = shifts_ref[...].reshape(1, 1, w)
    squares = shifts * shifts

    def spread_step(i, carry):
        cells = pltpu.roll(cells_ref[0 : 3 * bz, :], lax.rem(lanes - i * 2 * by, lanes), 1)
        for dx in range(2):
            k_field = 6.0 + field(cells, 0, dx, by, bz, w)
            c_field = field(cells, 1, dx, by, bz, w)
            m_field = field(cells, 2, dx, by, bz, w)
            spread[0, i * 2 + dx] = k_field
            spread[1, i * 2 + dx] = c_field
            spread[2, i * 2 + dx] = m_field
            diag[i * 2 + dx] = k_field + c_field * shifts + m_field * squares
        return carry

    lax.fori_loop(0, bx // 2, spread_step, 0)

    gather_start(0, g_src, g_recv, g_full)
    gather_end(0, g_full)
    (gram,) = matrices(1, g_full)
    for k, (exists, _, _, _, land) in enumerate(sides):
        @pl.when(exists)
        def _():
            halo_copy(k).start()

        @pl.when(jnp.logical_not(exists))
        def _():
            land[...] = jnp.zeros(land.shape, F32)
    upper, inverse = factorize(gram)
    factor_out[...] = upper / math.sqrt(all_cells)
    tiles = inv_tiles(inverse.T)

    def basis_step(i, total):
        at = pl.multiple_of(i * n_rows, n_rows)
        one = dot(ys[pl.ds(at, n_rows), : 2 * w], tiles[0])
        two = dot(ys[pl.ds(at, n_rows), w:], tiles[1])
        q = (two + one[:, w:]) + one[:, :w]
        pad[pl.ds(i * px + 1, px), 1 : by + 1] = q.reshape(px, by, bz, w)
        high, low = split(q)
        both = jnp.concatenate([high, low], axis=1)
        qs[pl.ds(at, n_rows), :] = both
        return total + dot_t(high, both)

    pair = lax.fori_loop(0, parts, basis_step, jnp.zeros((w, 2 * w), F32), unroll=True)
    small = pair[:, w:]
    reduce_start(1, [pair[:, :w] + (small + small.T)], h_src, h_recv)

    for k, (exists, _, _, _, _) in enumerate(sides):
        @pl.when(exists)
        def _():
            halo_copy(k).wait_send()
            halo_copy(k ^ 1).wait_recv()
    edges = [(pad.at[at, 1 : by + 1], halo_x.at[side]) for side, at in ((0, 0), (1, bx + 1))]
    edges += [(pad.at[1 : bx + 1, at], halo_y.at[side]) for side, at in ((0, 0), (1, by + 1))]
    spots, at = [], 0
    for land, halo in edges:
        size = halo.shape[0] * bz
        q = mm_six(halo[...].reshape(size, w), tiles)
        land[...] = q.reshape(halo.shape)
        hs[at : at + size, :] = jnp.concatenate(split(q), axis=1)
        spots.append((at, size))
        at += size
    for at_x in (0, bx + 1):
        for at_y in (0, by + 1):
            pad[at_x, at_y] = jnp.zeros((bz, w), F32)

    zero = jnp.zeros((by, 1, w), F32)
    proj[...] = jnp.zeros(proj.shape, F32)
    p_rows = 2 * by * bz

    def proj_step(i, carry):
        wides = []
        for dx in range(2):
            q, near = stencil(pad, i * 2 + dx, by, zero)
            k_block = spread[0, i * 2 + dx] * q - near
            c_block = spread[1, i * 2 + dx] * q
            m_block = spread[2, i * 2 + dx] * q + near * (1.0 / 12.0)
            wides.append(jnp.concatenate([v.reshape(by * bz, w) for v in (k_block, c_block, m_block)], axis=1))
        both = qs[pl.ds(pl.multiple_of(i * p_rows, p_rows), p_rows), :]
        qh, ql = both[:, :w], both[:, w:]
        vh, vl = split(jnp.concatenate(wides, axis=0))
        out = dot_t(ql, vh) + dot_t(qh, vl) + dot_t(qh, vh)
        for p in range(3):
            proj[p * w : (p + 1) * w, :] += out[:, p * w : (p + 1) * w]
        return carry

    steps = bx // 2
    cut = steps
    lax.fori_loop(0, cut, proj_step, 0, unroll=True)
    lax.fori_loop(cut, steps, proj_step, 0, unroll=True)
    reduce_start(2, [proj[p * w : (p + 1) * w, :] for p in range(3)], p_src, p_recv)
    gather_start(1, h_src, h_recv, h_full)
    gather_end(1, h_full)
    (gram,) = matrices(1, h_full)
    gather_start(2, p_src, p_recv, p_full)
    _, inverse = factorize(gram)
    inv_out[...] = inverse
    tile = coeff_tile(mm_t_three(inverse, ritz_ref[...]))

    def combine(both):
        out = dot(both, tile)
        return out[:, :w] + out[:, w:]

    for (at, size), (land, halo) in zip(spots, edges):
        land[...] = combine(hs[at : at + size, :]).reshape(halo.shape)
    for i in range(parts):
        v = combine(qs[i * n_rows : (i + 1) * n_rows, :]).reshape(px, by, bz, w)
        pad[i * px + 1 : (i + 1) * px + 1, 1 : by + 1] = v
        vec_out[i * px : (i + 1) * px] = v
    near_scale = squares * (1.0 / 12.0) - 1.0

    def residual_step(i, carry):
        for dx in range(2):
            v, near = stencil(pad, i * 2 + dx, by, zero)
            res_out[i * 2 + dx] = diag[i * 2 + dx] * v + near_scale * near
        return carry

    lax.fori_loop(0, bx // 2, residual_step, 0)
    drain(0, g_src, g_recv, g_full)
    drain(1, h_src, h_recv, h_full)
    gather_end(2, p_full)
    proj_out[...] = p_full[...]
    drain(2, p_src, p_recv, p_full)


def finish(
    vec_in, res_in, proj_in, inv_in, factor_in,
    vec_ref, res_ref, stiff_ref, damp_ref, mass_ref, factor_ref,
    made, sems,
):
    w = factor_ref.shape[0]
    pairs = [(vec_in, vec_ref), (res_in, res_ref), (factor_in, factor_ref)]
    pairs += [(made.at[p], ref) for p, ref in enumerate((stiff_ref, damp_ref, mass_ref))]
    copies = [pltpu.make_async_copy(a, b, sems.at[i]) for i, (a, b) in enumerate(pairs)]
    for copy in copies[:3]:
        copy.start()
    inverse = inv_in[...]
    half = mm(jnp.concatenate(matrices(3, proj_in), axis=0), inverse.T)
    out = mm(inverse, jnp.concatenate([half[p * w : (p + 1) * w] for p in range(3)], axis=1))
    for p in range(3):
        made[p] = out[:, p * w : (p + 1) * w]
        copies[3 + p].start()
    for copy in copies:
        copy.wait()


def local(sizes, moments, stiffness, damping, density, ritz_coeffs, shifts):
    nx, ny, nz, _ = sizes
    bx, by, bz, w = moments.shape
    owners = Owners(nx, ny, nz)
    devices, count = owners.devices, owners.count
    flat = [f.reshape(bx * by, bz) for f in (stiffness, damping, density)]
    r = -(-w // 2 // count) + 1
    mat = jax.ShapeDtypeStruct((w, w), F32)
    block = jax.ShapeDtypeStruct(moments.shape, F32)
    square = pltpu.VMEM((w, w), F32)
    hbm = pl.BlockSpec(memory_space=pltpu.HBM)
    vmem = pl.BlockSpec(memory_space=pltpu.VMEM)
    dma = pltpu.SemaphoreType.DMA
    padded = (bx + 2, by + 2, bz, w)

    def stages(rows):
        return [
            pltpu.VMEM((count, rows, w), F32),
            pltpu.VMEM((devices, rows, w), F32),
            pltpu.VMEM((count, rows, w), F32),
        ]

    shared = pl.pallas_call(
        functools.partial(kernel, sizes),
        out_shape=(
            pltpu.VMEM(moments.shape, F32), pltpu.VMEM(moments.shape, F32),
            pltpu.VMEM((count, 3 * r, w), F32), pltpu.VMEM((w, w), F32), pltpu.VMEM((w, w), F32),
        ),
        in_specs=[hbm] * 6,
        out_specs=(vmem,) * 5,
        scratch_shapes=[
            pltpu.VMEM(padded, F32),
            square,
            pltpu.VMEM((3 * w, w), F32),
            pltpu.VMEM(moments.shape, F32),
            pltpu.VMEM((bx * by * bz, 3 * w), BF16),
            pltpu.VMEM((bx * by * bz, 2 * w), BF16),
            pltpu.VMEM((2 * (bx + by) * bz, 2 * w), BF16),
            pltpu.VMEM((3, bx * by, bz), F32),
            pltpu.VMEM((3,) + moments.shape, F32),
            pltpu.VMEM(moments.shape, F32),
            square,
            pltpu.VMEM((1, w), F32),
            pltpu.VMEM((2, by, bz, w), F32),
            pltpu.VMEM((2, bx, bz, w), F32),
            *stages(r), *stages(r), *stages(3 * r),
            dma((9,)),
            dma((4,)), dma((4,)),
            dma((3, count)), dma((3, devices)),
            dma((3, devices)), dma((3, count)),
        ],
        compiler_params=pltpu.CompilerParams(
            collective_id=0, has_side_effects=True, vmem_limit_bytes=32 << 20
        ),
    )(*(pltpu.with_memory_space_constraint(a, pltpu.HBM) for a in (moments, *flat, ritz_coeffs, shifts.reshape(1, w))))
    any_space = pl.BlockSpec(memory_space=pl.ANY)
    return pl.pallas_call(
        finish,
        out_shape=(block, block, mat, mat, mat, mat),
        in_specs=[any_space, any_space, vmem, vmem, any_space],
        out_specs=(hbm,) * 6,
        scratch_shapes=[pltpu.VMEM((3, w, w), F32), dma((6,))],
        compiler_params=pltpu.CompilerParams(vmem_limit_bytes=8 << 20),
    )(*shared)


def solution(mesh):
    nx, ny, nz = (mesh.shape[a] for a in ("gx", "gy", "gz"))

    def call(moments, *rest):
        cells = moments.shape[0] * moments.shape[1] * moments.shape[2]
        body = functools.partial(local, (nx, ny, nz, cells * nx * ny * nz))
        return body(moments, *rest)

    cube = P("gx", ("gy", "gz"), None)
    block = P("gx", ("gy", "gz"), None, None)
    return jax.shard_map(
        call,
        mesh=mesh,
        in_specs=(block, cube, cube, cube, P(), P()),
        out_specs=(block, block, P(), P(), P(), P()),
        check_vma=False,
    )
```

```python
import functools
import math
import jax
import jax.numpy as jnp
from jax import lax
from jax.experimental import pallas as pl
from jax.experimental.pallas import tpu as pltpu
from jax.sharding import PartitionSpec as P

MESH = pl.DeviceIdType.MESH
HI = lax.Precision.HIGHEST
F32 = jnp.float32
BF16 = jnp.bfloat16
BLK = 32
PANEL = 16


def mm(a, b):
    return lax.dot_general(a, b, (((1,), (0,)), ((), ())), precision=HI, preferred_element_type=F32)


def split(x):
    high = x.astype(BF16)
    return high, (x - high.astype(F32)).astype(BF16)


def split3(x):
    high = x.astype(BF16)
    rest = x - high.astype(F32)
    mid = rest.astype(BF16)
    return high, mid, (rest - mid.astype(F32)).astype(BF16)


def dot_t(a, b):
    return lax.dot_general(a, b, (((0,), (0,)), ((), ())), preferred_element_type=F32)


def dot(a, b):
    return lax.dot_general(a, b, (((1,), (0,)), ((), ())), preferred_element_type=F32)


def rank_update(a, b):
    ah, am, al = split3(a)
    bh, bm, bl = split3(b)
    left = jnp.concatenate([ah, am, ah, am, ah, al], axis=0)
    right = jnp.concatenate([bh, bh, bm, bm, bl, bh], axis=0)
    return dot_t(left, right)


def mm_t_three(a, b):
    ah, al = split(a)
    bh, bl = split(b)
    return dot_t(jnp.concatenate([ah, ah, al], axis=0), jnp.concatenate([bh, bl, bh], axis=0))


def coeff_tile(c):
    high, low = split(c)
    return jnp.concatenate(
        [jnp.concatenate([high, low], axis=1), jnp.concatenate([high, jnp.zeros_like(high)], axis=1)], axis=0
    )


def inv_tiles(c):
    high, mid, low = split3(c)
    pair = jnp.concatenate([high, mid], axis=1)
    return jnp.concatenate([pair, pair], axis=0), jnp.concatenate([low, high], axis=0)


def mm_six(rows, tiles):
    w = rows.shape[1]
    high, mid, low = split3(rows)
    one = dot(jnp.concatenate([high, mid], axis=1), tiles[0])
    two = dot(jnp.concatenate([high, low], axis=1), tiles[1])
    return (two + one[:, w:]) + one[:, :w]


def stencil(pad, x, by, zero):
    q = pad[x + 1, 1 : by + 1]
    near = pad[x, 1 : by + 1] + pad[x + 2, 1 : by + 1]
    near = near + pad[x + 1, 0:by] + pad[x + 1, 2 : by + 2]
    near = near + jnp.concatenate([q[:, 1:], zero], axis=1)
    near = near + jnp.concatenate([zero, q[:, :-1]], axis=1)
    return q, near


def field(cells, f, dx, by, bz, w):
    part = cells[f * bz : (f + 1) * bz]
    return jnp.stack([jnp.broadcast_to(part[:, dx * by + y : dx * by + y + 1], (bz, w)) for y in range(by)])


def eliminate(a, first):
    nr, n = a.shape
    lane = lax.broadcasted_iota(jnp.int32, (nr, n), 1)
    row = lax.broadcasted_iota(jnp.int32, (nr, n), 0)
    cols = [jnp.broadcast_to(a[:, first + k : first + k + 1], (nr, n)) for k in range(PANEL)]
    inside = (lane >= first) & (lane < first + PANEL)
    rest = jnp.where(inside, jnp.where(lane == first + row, 1.0, 0.0), a)
    lane, sub = lane[:PANEL], row[:PANEL]
    recips = jnp.zeros((PANEL, n), F32)
    for s in range(PANEL):
        recip = 1.0 / cols[s][s : s + 1]
        recips = jnp.where(sub == s, recip, recips)
        if s == nr - 1:
            break
        m = jnp.where(row > s, cols[s], 0.0) * recip
        for k in range(s + 1, PANEL):
            cols[k] = cols[k] - m * cols[k][s : s + 1]
        rest = rest - m * rest[s : s + 1]
    done = rest[:PANEL]
    e = jnp.where(lane < first + PANEL, done, 0.0)
    u = jnp.where(lane >= first + PANEL, done, 0.0)
    for k in range(PANEL):
        u = jnp.where((lane == first + k) & (sub <= k), cols[k][:PANEL], u)
    return u, e, recips, rest[PANEL:]


def factorize(g, between=None):
    n = g.shape[0]
    blocks = n // BLK
    rows = [g[b * BLK : (b + 1) * BLK] for b in range(blocks)]
    upper, inverse = [], []
    lane = lax.broadcasted_iota(jnp.int32, (BLK, n), 1)
    for j in range(blocks):
        first = j * BLK
        a = rows[j]
        parts = []
        for p in range(BLK // PANEL):
            u, e, recips, a = eliminate(a, first + p * PANEL)
            parts.append((u, e, recips))
        u, e, recips = (jnp.concatenate(x, axis=0) for x in zip(*parts))
        if j < blocks - 1:
            beyond = jnp.where(lane >= first + BLK, u, 0.0)
            update = rank_update(beyond * recips, beyond + e)
            inside = (lane >= first) & (lane < first + BLK)
            for b in range(j + 1, blocks):
                rows[b] = jnp.where(inside, 0.0, rows[b]) - update[b * BLK : (b + 1) * BLK]
        scale = jnp.sqrt(recips)
        upper.append(u * scale)
        inverse.append(e * scale)
        if between and j == 0:
            between()
    return jnp.concatenate(upper, axis=0), jnp.concatenate(inverse, axis=0)


def halves(h, w):
    row = lax.broadcasted_iota(jnp.int32, (h, w), 0)
    lane = lax.broadcasted_iota(jnp.int32, (h, w), 1)
    return row, lane


def pack(g):
    w = g.shape[0]
    h = w // 2
    row, lane = halves(h, w)
    top, low = g[:h], g[h:]
    turned = pltpu.roll(low, h, 1)
    body = jnp.where((lane >= h) | (row >= lane), top, turned)
    ends = jnp.where(row == lane, turned, 0.0) + jnp.where(row == lane - h, low, 0.0)
    return body, jnp.sum(ends, axis=0, keepdims=True)


def unpack(body, ends):
    h, w = body.shape
    row, lane = halves(h, w)
    flipped = jnp.concatenate([body, body], axis=0).T
    top = jnp.where((lane >= h) | (row >= lane), body, flipped[:h])
    last = jnp.where(row == lane - h, jnp.broadcast_to(ends, (h, w)), flipped[:h])
    last = jnp.where(row < lane - h, pltpu.roll(body, h, 1), last)
    return jnp.concatenate([top, jnp.where(lane < h, flipped[h:], last)], axis=0)


def matrices(k, full):
    count = full.shape[0]
    r = full.shape[1] // k - 1
    out = []
    for p in range(k):
        body = jnp.concatenate([full[o, p * r : (p + 1) * r, :] for o in range(count)], axis=0)
        out.append(unpack(body[: body.shape[1] // 2], full[0, k * r + p : k * r + p + 1, :]))
    return out


def each(n, fn):
    if n <= 64:
        for g in range(n):
            fn(g)
    else:
        def step(g, carry):
            fn(g)
            return carry

        lax.fori_loop(0, n, step, 0)


def add_up(terms):
    while len(terms) > 1:
        pairs = [terms[i] + terms[i + 1] for i in range(0, len(terms) - 1, 2)]
        terms = pairs + terms[len(pairs) * 2 :]
    return terms[0]


class Owners:
    def __init__(self, nx, ny, nz):
        stride = 2 if nz % 2 == 0 else 1
        span = 2 if ny % 2 == 0 else 1
        first = (ny - span) // 2
        self.nz, self.group = nz, nx * nz
        self.devices = self.group * ny
        table = [
            plane * self.group + a
            for plane in range(first, first + span)
            for a in range(stride - 1, self.group, stride)
        ]
        self.table = table[1:-1] if len(table) > 4 else table
        self.count = len(self.table)

    def holds(self, me):
        held = me == self.table[0]
        for g in self.table[1:]:
            held = held | (me == g)
        return held

    def part(self, me):
        part = jnp.int32(0)
        for o, g in enumerate(self.table):
            part = part + jnp.where(me == g, o, 0)
        return part

    def device(self, o):
        return self.table[o]

    def place(self, g):
        a = g % self.group
        return (a // self.nz, g // self.group, a % self.nz)


def kernel(
    sizes,
    y_hbm, stiff_in, damp_in, dens_in, ritz_in, shifts_in,
    vec_out, res_out, proj_out, inv_out, factor_out,
    pad, cells_ref, proj,
    y_ref, ys, qs, hs, fields, spread, diag, ritz_ref, shifts_ref, halo_x, halo_y,
    g_src, g_recv, g_full, h_src, h_recv, h_full, p_src, p_recv, p_full, load_sem,
    halo_send, halo_got, a_send, a_got, b_send, b_got,
):
    nx, ny, nz, all_cells = sizes
    bx, by, bz, w = y_ref.shape
    ix, iy, iz = lax.axis_index("gx"), lax.axis_index("gy"), lax.axis_index("gz")
    owners = Owners(nx, ny, nz)
    devices, count = owners.devices, owners.count
    mine = ix * nz + iz
    me = iy * owners.group + mine
    line = iy * nz + iz
    is_owner = owners.holds(me)
    my_part = owners.part(me)

    def line_id(a):
        return (ix, lax.div(a, nz), lax.rem(a, nz))

    sides = [
        (ix > 0, (ix - 1, iy, iz), y_ref.at[0], halo_x.at[1], halo_x.at[0]),
        (ix < nx - 1, (ix + 1, iy, iz), y_ref.at[bx - 1], halo_x.at[0], halo_x.at[1]),
        (line > 0, line_id(line - 1), y_ref.at[:, 0], halo_y.at[1], halo_y.at[0]),
        (line < ny * nz - 1, line_id(line + 1), y_ref.at[:, by - 1], halo_y.at[0], halo_y.at[1]),
    ]

    parts = 2
    px = bx // parts
    loads = [
        pltpu.make_async_copy(y_hbm.at[pl.ds(i * px, px)], y_ref.at[pl.ds(i * px, px)], load_sem.at[i])
        for i in range(parts)
    ]
    for f, src in enumerate((stiff_in, damp_in, dens_in)):
        loads.append(pltpu.make_async_copy(src, fields.at[f], load_sem.at[parts + f]))
    loads.append(pltpu.make_async_copy(ritz_in, ritz_ref, load_sem.at[parts + 3]))
    loads.append(pltpu.make_async_copy(shifts_in, shifts_ref, load_sem.at[parts + 4]))
    for load in loads:
        load.start()

    barrier = pltpu.get_barrier_semaphore()
    def greet(g):
        pl.semaphore_signal(barrier, inc=1, device_id=owners.place(g), device_id_type=MESH)

    def greet_owner(o):
        @pl.when(me != owners.device(o))
        def _():
            greet(owners.device(o))

    def greet_all(g):
        @pl.when(me != g)
        def _():
            greet(g)

    @pl.when(is_owner)
    def _():
        each(devices, greet_all)

    @pl.when(jnp.logical_not(is_owner))
    def _():
        each(count, greet_owner)

    expected = jnp.where(is_owner, devices - 1, count)
    for exists, device, _, _, _ in sides:
        expected = expected + exists.astype(jnp.int32)

        @pl.when(exists)
        def _():
            pl.semaphore_signal(barrier, inc=1, device_id=device, device_id_type=MESH)

    cross = jnp.zeros((2 * w, 2 * w), F32)
    third_order = jnp.zeros((w, w), F32)
    n_rows = px * by * bz
    for i in range(parts):
        loads[i].wait()
        high, mid, low = split3(y_ref[i * px : (i + 1) * px].reshape(n_rows, w))
        two = jnp.concatenate([mid, high], axis=1)
        ys[i * n_rows : (i + 1) * n_rows, : 2 * w] = two
        ys[i * n_rows : (i + 1) * n_rows, 2 * w :] = low
        cross = cross + dot_t(two, two)
        third_order = third_order + dot_t(high, low)
    small = cross[:w, w:] + third_order
    gram = cross[w:, w:] + (cross[:w, :w] + (small + small.T))

    pl.semaphore_wait(barrier, expected)

    def halo_copy(k):
        _, device, src, dst, _ = sides[k]
        other = k ^ 1
        return pltpu.make_async_remote_copy(
            src_ref=src, dst_ref=dst, send_sem=halo_send.at[k], recv_sem=halo_got.at[other],
            device_id=device, device_id_type=MESH,
        )

    def to_owner(slot, o, src, recv, sender):
        return pltpu.make_async_remote_copy(
            src_ref=src.at[o], dst_ref=recv.at[sender], send_sem=a_send.at[slot, o],
            recv_sem=a_got.at[slot, sender], device_id=owners.place(owners.device(o)), device_id_type=MESH,
        )

    def from_owner(slot, g, full, part):
        return pltpu.make_async_remote_copy(
            src_ref=full.at[part], dst_ref=full.at[part], send_sem=b_send.at[slot, g],
            recv_sem=b_got.at[slot, part], device_id=owners.place(g), device_id_type=MESH,
        )

    def each_owner(fn):
        def other(o):
            @pl.when(me != owners.device(o))
            def _():
                fn(o)

        each(count, other)

    def each_device(fn):
        def other(g):
            @pl.when(me != g)
            def _():
                fn(g)

        each(devices, other)

    def reduce_start(slot, mats, src, recv):
        k = len(mats)
        r = src.shape[1] // k - 1
        for p, mat in enumerate(mats):
            body, ends = pack(mat)
            spare = r * count - body.shape[0]
            if spare:
                body = jnp.concatenate([body, jnp.zeros((spare, w), F32)], axis=0)
            for o in range(count):
                src[o, p * r : (p + 1) * r, :] = body[o * r : (o + 1) * r]
                src[o, k * r + p : k * r + p + 1, :] = ends
        each_owner(lambda o: to_owner(slot, o, src, recv, me).start())

    def gather_start(slot, src, recv, full):
        @pl.when(is_owner)
        def _():
            recv[me] = src[my_part]
            each_device(lambda g: to_owner(slot, 0, src, recv, g).wait_recv())
            full[my_part] = add_up([recv[g] for g in range(devices)])
            each_device(lambda g: from_owner(slot, g, full, my_part).start())

    def gather_end(slot, full):
        each_owner(lambda o: from_owner(slot, 0, full, o).wait_recv())

    def drain(slot, src, recv, full):
        each_owner(lambda o: to_owner(slot, o, src, recv, me).wait_send())

        @pl.when(is_owner)
        def _():
            each_device(lambda g: from_owner(slot, g, full, my_part).wait_send())

    reduce_start(0, [gram], g_src, g_recv)

    empty = jnp.zeros((bx * by, w - 3 * bz), F32)
    for load in loads[parts:]:
        load.wait()
    cells_ref[...] = jnp.concatenate([fields[0], fields[1], fields[2], empty], axis=1).T
    lanes = bx * by
    shifts = shifts_ref[...].reshape(1, 1, w)
    squares = shifts * shifts

    def spread_step(i, carry):
        cells = pltpu.roll(cells_ref[0 : 3 * bz, :], lax.rem(lanes - i * 2 * by, lanes), 1)
        for dx in range(2):
            k_field = 6.0 + field(cells, 0, dx, by, bz, w)
            c_field = field(cells, 1, dx, by, bz, w)
            m_field = field(cells, 2, dx, by, bz, w)
            spread[0, i * 2 + dx] = k_field
            spread[1, i * 2 + dx] = c_field
            spread[2, i * 2 + dx] = m_field
            diag[i * 2 + dx] = k_field + c_field * shifts + m_field * squares
        return carry

    lax.fori_loop(0, bx // 2, spread_step, 0)

    gather_start(0, g_src, g_recv, g_full)
    gather_end(0, g_full)
    (gram,) = matrices(1, g_full)
    for k, (exists, _, _, _, land) in enumerate(sides):
        @pl.when(exists)
        def _():
            halo_copy(k).start()

        @pl.when(jnp.logical_not(exists))
        def _():
            land[...] = jnp.zeros(land.shape, F32)
    upper, inverse = factorize(gram)
    factor_out[...] = upper / math.sqrt(all_cells)
    tiles = inv_tiles(inverse.T)

    def basis_step(i, total):
        at = pl.multiple_of(i * n_rows, n_rows)
        one = dot(ys[pl.ds(at, n_rows), : 2 * w], tiles[0])
        two = dot(ys[pl.ds(at, n_rows), w:], tiles[1])
        q = (two + one[:, w:]) + one[:, :w]
        pad[pl.ds(i * px + 1, px), 1 : by + 1] = q.reshape(px, by, bz, w)
        high, low = split(q)
        both = jnp.concatenate([high, low], axis=1)
        qs[pl.ds(at, n_rows), :] = both
        return total + dot_t(high, both)

    pair = lax.fori_loop(0, parts, basis_step, jnp.zeros((w, 2 * w), F32), unroll=True)
    small = pair[:, w:]
    reduce_start(1, [pair[:, :w] + (small + small.T)], h_src, h_recv)

    for k, (exists, _, _, _, _) in enumerate(sides):
        @pl.when(exists)
        def _():
            halo_copy(k).wait_send()
            halo_copy(k ^ 1).wait_recv()
    edges = [(pad.at[at, 1 : by + 1], halo_x.at[side]) for side, at in ((0, 0), (1, bx + 1))]
    edges += [(pad.at[1 : bx + 1, at], halo_y.at[side]) for side, at in ((0, 0), (1, by + 1))]
    spots, at = [], 0
    for land, halo in edges:
        size = halo.shape[0] * bz
        q = mm_six(halo[...].reshape(size, w), tiles)
        land[...] = q.reshape(halo.shape)
        hs[at : at + size, :] = jnp.concatenate(split(q), axis=1)
        spots.append((at, size))
        at += size
    for at_x in (0, bx + 1):
        for at_y in (0, by + 1):
            pad[at_x, at_y] = jnp.zeros((bz, w), F32)

    zero = jnp.zeros((by, 1, w), F32)
    proj[...] = jnp.zeros(proj.shape, F32)
    p_rows = 4 * by * bz

    def proj_step(i, carry):
        wides = []
        for dx in range(4):
            q, near = stencil(pad, i * 4 + dx, by, zero)
            k_block = spread[0, i * 4 + dx] * q - near
            c_block = spread[1, i * 4 + dx] * q
            m_block = spread[2, i * 4 + dx] * q + near * (1.0 / 12.0)
            wides.append(jnp.concatenate([v.reshape(by * bz, w) for v in (k_block, c_block, m_block)], axis=1))
        both = qs[pl.ds(pl.multiple_of(i * p_rows, p_rows), p_rows), :]
        qh, ql = both[:, :w], both[:, w:]
        vh, vl = split(jnp.concatenate(wides, axis=0))
        out = dot_t(ql, vh) + dot_t(qh, vl) + dot_t(qh, vh)
        for p in range(3):
            proj[p * w : (p + 1) * w, :] += out[:, p * w : (p + 1) * w]
        return carry

    steps = bx // 4
    cut = steps
    lax.fori_loop(0, cut, proj_step, 0, unroll=True)
    lax.fori_loop(cut, steps, proj_step, 0, unroll=True)
    reduce_start(2, [proj[p * w : (p + 1) * w, :] for p in range(3)], p_src, p_recv)
    drain(0, g_src, g_recv, g_full)
    gather_start(1, h_src, h_recv, h_full)
    gather_end(1, h_full)
    (gram,) = matrices(1, h_full)
    gather_start(2, p_src, p_recv, p_full)
    _, inverse = factorize(gram)
    inv_out[...] = inverse
    tile = coeff_tile(mm_t_three(inverse, ritz_ref[...]))

    def combine(both):
        out = dot(both, tile)
        return out[:, :w] + out[:, w:]

    for (at, size), (land, halo) in zip(spots, edges):
        land[...] = combine(hs[at : at + size, :]).reshape(halo.shape)
    for i in range(parts):
        v = combine(qs[i * n_rows : (i + 1) * n_rows, :]).reshape(px, by, bz, w)
        pad[i * px + 1 : (i + 1) * px + 1, 1 : by + 1] = v
        vec_out[i * px : (i + 1) * px] = v
    near_scale = squares * (1.0 / 12.0) - 1.0

    def residual_step(i, carry):
        for dx in range(2):
            v, near = stencil(pad, i * 2 + dx, by, zero)
            res_out[i * 2 + dx] = diag[i * 2 + dx] * v + near_scale * near
        return carry

    lax.fori_loop(0, bx // 2, residual_step, 0)
    drain(1, h_src, h_recv, h_full)
    gather_end(2, p_full)
    proj_out[...] = p_full[...]
    drain(2, p_src, p_recv, p_full)


def finish(
    vec_in, res_in, proj_in, inv_in, factor_in,
    vec_ref, res_ref, stiff_ref, damp_ref, mass_ref, factor_ref,
    made, sems,
):
    w = factor_ref.shape[0]
    pairs = [(vec_in, vec_ref), (res_in, res_ref), (factor_in, factor_ref)]
    pairs += [(made.at[p], ref) for p, ref in enumerate((stiff_ref, damp_ref, mass_ref))]
    copies = [pltpu.make_async_copy(a, b, sems.at[i]) for i, (a, b) in enumerate(pairs)]
    for copy in copies[:3]:
        copy.start()
    inverse = inv_in[...]
    half = mm(jnp.concatenate(matrices(3, proj_in), axis=0), inverse.T)
    out = mm(inverse, jnp.concatenate([half[p * w : (p + 1) * w] for p in range(3)], axis=1))
    for p in range(3):
        made[p] = out[:, p * w : (p + 1) * w]
        copies[3 + p].start()
    for copy in copies:
        copy.wait()


def local(sizes, moments, stiffness, damping, density, ritz_coeffs, shifts):
    nx, ny, nz, _ = sizes
    bx, by, bz, w = moments.shape
    owners = Owners(nx, ny, nz)
    devices, count = owners.devices, owners.count
    flat = [f.reshape(bx * by, bz) for f in (stiffness, damping, density)]
    r = -(-w // 2 // count) + 1
    mat = jax.ShapeDtypeStruct((w, w), F32)
    block = jax.ShapeDtypeStruct(moments.shape, F32)
    square = pltpu.VMEM((w, w), F32)
    hbm = pl.BlockSpec(memory_space=pltpu.HBM)
    vmem = pl.BlockSpec(memory_space=pltpu.VMEM)
    dma = pltpu.SemaphoreType.DMA
    padded = (bx + 2, by + 2, bz, w)

    def stages(rows):
        return [
            pltpu.VMEM((count, rows, w), F32),
            pltpu.VMEM((devices, rows, w), F32),
            pltpu.VMEM((count, rows, w), F32),
        ]

    shared = pl.pallas_call(
        functools.partial(kernel, sizes),
        out_shape=(
            pltpu.VMEM(moments.shape, F32), pltpu.VMEM(moments.shape, F32),
            pltpu.VMEM((count, 3 * r, w), F32), pltpu.VMEM((w, w), F32), pltpu.VMEM((w, w), F32),
        ),
        in_specs=[hbm] * 6,
        out_specs=(vmem,) * 5,
        scratch_shapes=[
            pltpu.VMEM(padded, F32),
            square,
            pltpu.VMEM((3 * w, w), F32),
            pltpu.VMEM(moments.shape, F32),
            pltpu.VMEM((bx * by * bz, 3 * w), BF16),
            pltpu.VMEM((bx * by * bz, 2 * w), BF16),
            pltpu.VMEM((2 * (bx + by) * bz, 2 * w), BF16),
            pltpu.VMEM((3, bx * by, bz), F32),
            pltpu.VMEM((3,) + moments.shape, F32),
            pltpu.VMEM(moments.shape, F32),
            square,
            pltpu.VMEM((1, w), F32),
            pltpu.VMEM((2, by, bz, w), F32),
            pltpu.VMEM((2, bx, bz, w), F32),
            *stages(r), *stages(r), *stages(3 * r),
            dma((9,)),
            dma((4,)), dma((4,)),
            dma((3, count)), dma((3, devices)),
            dma((3, devices)), dma((3, count)),
        ],
        compiler_params=pltpu.CompilerParams(
            collective_id=0, has_side_effects=True, vmem_limit_bytes=32 << 20
        ),
    )(*(pltpu.with_memory_space_constraint(a, pltpu.HBM) for a in (moments, *flat, ritz_coeffs, shifts.reshape(1, w))))
    any_space = pl.BlockSpec(memory_space=pl.ANY)
    return pl.pallas_call(
        finish,
        out_shape=(block, block, mat, mat, mat, mat),
        in_specs=[any_space, any_space, vmem, vmem, any_space],
        out_specs=(hbm,) * 6,
        scratch_shapes=[pltpu.VMEM((3, w, w), F32), dma((6,))],
        compiler_params=pltpu.CompilerParams(vmem_limit_bytes=8 << 20),
    )(*shared)


def solution(mesh):
    nx, ny, nz = (mesh.shape[a] for a in ("gx", "gy", "gz"))

    def call(moments, *rest):
        cells = moments.shape[0] * moments.shape[1] * moments.shape[2]
        body = functools.partial(local, (nx, ny, nz, cells * nx * ny * nz))
        return body(moments, *rest)

    cube = P("gx", ("gy", "gz"), None)
    block = P("gx", ("gy", "gz"), None, None)
    return jax.shard_map(
        call,
        mesh=mesh,
        in_specs=(block, cube, cube, cube, P(), P()),
        out_specs=(block, block, P(), P(), P(), P()),
        check_vma=False,
    )
```
